32 devices in a mesh: batch: 2 (over core), ctx: 4 (over z), tensor: 4 (over y, x).
Axes of the slice: x: 2, y: 2, z: 4, core: 2. Of those that a mesh axis runs over, the one named last changes fastest.
Arguments:
- hidden_in: bfloat16 [2, 2, 512, 2048], P(None, 'batch', 'ctx'), may hold values from -6 to 6
- segment_ids: int32 [2, 2, 512], P(None, 'batch', 'ctx'), may hold values from 0 to 3, never falling along the last dimension, each value on 1 to 256 neighbouring positions
- expert_ids: int32 [2, 2, 512, 8], P(None, 'batch', 'ctx'), may hold values from 0 to 31, as said below
- capacity: int32 [32], replicated, may hold values from 128 to 320, as said below
- norm_attn: float32 [2048], replicated, may hold values from 0.25 to 1.75
- norm_ffn: float32 [2048], replicated, may hold values from 0.25 to 1.75
- norm_query: float32 [128], replicated, may hold values from 0.25 to 1.75
- norm_key: float32 [128], replicated, may hold values from 0.25 to 1.75
- w_query: bfloat16 [2048, 4096], P(('batch', 'ctx'), 'tensor'), may hold values from -0.125 to 0.125
- w_key: bfloat16 [2048, 512], P(('batch', 'ctx'), 'tensor'), may hold values from -0.125 to 0.125
- w_value: bfloat16 [2048, 512], P(('batch', 'ctx'), 'tensor'), may hold values from -0.125 to 0.125
- w_out: bfloat16 [2048, 4096], P(('batch', 'ctx'), 'tensor'), may hold values from -0.75 to 0.75
- w_router: bfloat16 [2048, 32], P(('batch', 'ctx')), may hold values from -0.0625 to 0.0625
- w_gate: bfloat16 [32, 768, 2048], P(('batch', 'ctx'), 'tensor'), may hold values from -0.125 to 0.125
- w_up: bfloat16 [32, 768, 2048], P(('batch', 'ctx'), 'tensor'), may hold values from -0.125 to 0.125
- w_down: bfloat16 [32, 768, 2048], P(('batch', 'ctx'), 'tensor'), may hold values from -1.25 to 1.25
- grad_out: bfloat16 [2, 2, 512, 2048], P(None, 'batch', 'ctx'), may hold values from -6 to 6
Outputs:
- hidden_out: float32 [2, 2, 512, 2048], P(None, 'batch', 'ctx')
- grad_in: float32 [2, 2, 512, 2048], P(None, 'batch', 'ctx')
- grad_norm_attn: float32 [2048], P(('batch', 'ctx'))
- grad_norm_ffn: float32 [2048], P(('batch', 'ctx'))
- grad_norm_query: float32 [128], P(('batch', 'ctx'))
- grad_norm_key: float32 [128], P(('batch', 'ctx'))
- grad_query: float32 [2048, 4096], P(('batch', 'ctx'), 'tensor')
- grad_key: float32 [2048, 512], P(('batch', 'ctx'), 'tensor')
- grad_value: float32 [2048, 512], P(('batch', 'ctx'), 'tensor')
- grad_out_proj: float32 [2048, 4096], P(('batch', 'ctx'), 'tensor')
- grad_router: float32 [2048, 32], P(('batch', 'ctx'))
- grad_gate: float32 [32, 768, 2048], P(('batch', 'ctx'), 'tensor')
- grad_up: float32 [32, 768, 2048], P(('batch', 'ctx'), 'tensor')
- grad_down: float32 [32, 768, 2048], P(('batch', 'ctx'), 'tensor')
The draws below stay inside these ranges and needn't reach their ends.
Inputs may be any that keep to these rules, and one draw needn't show every extreme that they name: `expert_ids`: each row names 8 different experts; among the 128 rows of one device of one micro-batch a quarter of the experts are named exactly 64 times, a quarter exactly 64 / 2 times and the rest exactly 64 / 4 times. `segment_ids`: ids never fall along a sequence; a document holds at most 256 tokens. `capacity`: the most pairs of one micro-batch that an expert keeps.
All inputs are finite; a program needn't handle non-finite values.
Results may differ from the reference program's by a relative error of at most 0.028.
Values may be sent and summed in bfloat16 or wider, within the bound.
No kernel may reach another device: no remote copies, remote signals or barrier semaphores. Data moves between devices by JAX's collectives and lax.ppermute only.
A program may use at most 320 MiB of HBM per device.

```python
import math
import jax
import jax.numpy as jnp
import numpy as np
from jax import lax

D = 2048
H = 32
KVH = 4
HD = 128
FF = 768
TOPK = 8
SPAN = 128
MICRO = 2
SEQS = 2
SEQ = 512
EXPERTS = 32
MOST = 64
LOAD = 256
CAP = 320
DOC_MOST = 256
DOCS = 4
N_TENSOR = 4


def draw_capacity(key, part):
    first_key, second_key = jax.random.split(jax.random.fold_in(key, 11))
    levels = jax.random.randint(first_key, (EXPERTS,), LOAD // 2, CAP + 1)
    marked = jax.random.randint(second_key, (), 0, EXPERTS)
    return jnp.where(jnp.arange(EXPERTS) == marked, CAP, levels).astype(jnp.int32)


def draw_expert_ids(key, part):
    pop_key, noise_key, token_key, slot_key = jax.random.split(jax.random.fold_in(key, 23), 4)
    per_micro = SEQS * (SEQ // SPAN)
    block_count = MICRO * per_micro
    popularity = jax.random.randint(pop_key, (MICRO, 1, EXPERTS), 0, 4)
    noise = jax.random.randint(noise_key, (MICRO, per_micro, EXPERTS), 0, 1536)
    scores = (popularity * 1024 + noise) * EXPERTS + jnp.arange(EXPERTS, dtype=jnp.int32)[None, None, :]
    order = jnp.argsort(-scores, axis=-1).reshape(block_count, EXPERTS).astype(jnp.int32)
    pair_count = SPAN * TOPK
    position = jnp.arange(pair_count, dtype=jnp.int32)
    quarter = EXPERTS // 4
    first_end = quarter * MOST
    second_end = first_end + quarter * (MOST // 2)
    rank_index = jnp.where(position < first_end, position // MOST, jnp.where(position < second_end, quarter + (position - first_end) // (MOST // 2), 2 * quarter + (position - second_end) // (MOST // 4))).astype(jnp.int32)
    listed = jnp.take(order, rank_index, axis=1)
    table = listed.reshape(block_count, TOPK, SPAN).transpose(0, 2, 1)
    token_scores = jax.random.randint(token_key, (block_count, SPAN), 0, 1048576) * SPAN + jnp.arange(SPAN, dtype=jnp.int32)[None, :]
    token_order = jnp.argsort(token_scores, axis=-1).astype(jnp.int32)
    table = jnp.take_along_axis(table, token_order[:, :, None], axis=1)
    slot_scores = jax.random.randint(slot_key, (block_count, SPAN, TOPK), 0, 1048576) * TOPK + jnp.arange(TOPK, dtype=jnp.int32)[None, None, :]
    slot_order = jnp.argsort(slot_scores, axis=-1).astype(jnp.int32)
    table = jnp.take_along_axis(table, slot_order, axis=2)
    return table.reshape(MICRO, SEQS, SEQ, TOPK).astype(jnp.int32)


def shard_levels(key, dims, cuts, low, largest):
    factor_of = 1.0
    for dim, parts in cuts:
        draws = jax.random.uniform(jax.random.fold_in(jax.random.fold_in(key, 6), dim), (parts,), jnp.float32, low / len(cuts), largest / len(cuts))
        factor_of = factor_of * jnp.repeat(jnp.exp(draws), dims[dim] // parts).reshape((-1,) + (1,) * (len(dims) - 1 - dim))
    return factor_of


def profile(number_of, total, reach, lean):
    portions = [(1 << 20) // math.isqrt(standing ** lean) + 1 for standing in range(2, number_of + 1)]
    rest, holding = total - reach - (number_of - 1), [1] * (number_of - 1)
    while rest > 0:
        candidates = [i for i in range(number_of - 1) if holding[i] < reach]
        pool, remaining = sum([portions[i] for i in candidates]), rest
        for i in candidates:
            extra = min(reach - holding[i], max(1, remaining * portions[i] // pool), rest)
            holding[i] = holding[i] + extra
            rest = rest - extra
    return np.array([reach] + holding)


def uneven_parts(rng, number_of, total, reach, lean):
    if number_of == 2:
        one = jax.random.randint(rng, (), max(1, total - reach), min(reach, total - 1) + 1)
        return jnp.stack([one, total - one])
    lengths = jnp.asarray(profile(number_of, total, reach, lean), jnp.int32)
    couples = (number_of - 1) // 2
    source_of, taker = lengths[1:1 + 2 * couples:2], lengths[2:2 + 2 * couples:2]
    margin = jnp.minimum(source_of - 1, reach - taker)
    shifted = jax.random.randint(jax.random.fold_in(rng, 1), (couples,), 0, 1 << 20) % (margin + 1)
    lengths = lengths.at[1:1 + 2 * couples:2].set(source_of - shifted).at[2:2 + 2 * couples:2].set(taker + shifted)
    return lengths[jax.random.permutation(jax.random.fold_in(rng, 2), number_of)]


def normal_values(rng, extent, scale, most, shards=(), kind=jnp.bfloat16):
    entries = jax.random.normal(rng, extent, jnp.float32) * scale
    if len(shards) > 0:
        entries = shard_levels(rng, extent, shards, -0.22, 0.18) * entries
    return jnp.clip(entries, min=-most, max=most).astype(kind)


def setup_inputs(seed: int = 0) -> dict:
    keys = jax.random.split(jax.random.key(seed), 18)
    hidden_in = normal_values(keys[0], (MICRO, SEQS, SEQ, D), 1.0, 6.0, ((1, 2), (2, 4)))
    segment_ids = jax.vmap(lambda own: jnp.searchsorted(jnp.cumsum(uneven_parts(own, DOCS, SEQ, DOC_MOST, 1)), jnp.arange(SEQ), side="right"))(jax.random.split(keys[1], MICRO * SEQS)).reshape((MICRO, SEQS, SEQ)).astype(jnp.int32)
    expert_ids = draw_expert_ids(jax.random.fold_in(keys[17], 71), 0)
    capacity = draw_capacity(jax.random.fold_in(keys[17], 71), 0)
    norm_attn = jnp.clip(1.0 + 0.15 * jax.random.normal(keys[4], (D,), jnp.float32), 0.25, 1.75)
    norm_ffn = jnp.clip(1.0 + 0.15 * jax.random.normal(keys[5], (D,), jnp.float32), 0.25, 1.75)
    norm_query = jnp.clip(1.0 + 0.15 * jax.random.normal(keys[6], (HD,), jnp.float32), 0.25, 1.75)
    norm_key = jnp.clip(1.0 + 0.15 * jax.random.normal(keys[7], (HD,), jnp.float32), 0.25, 1.75)
    w_query = normal_values(keys[8], (D, H * HD), D ** -0.5, 0.125, ((0, 8), (1, 4)))
    w_key = normal_values(keys[9], (D, KVH * HD), D ** -0.5, 0.125, ((0, 8), (1, 4)))
    w_value = normal_values(keys[10], (D, KVH * HD), D ** -0.5, 0.125, ((0, 8), (1, 4)))
    w_out = normal_values(keys[11], (D, H * HD), (H * HD // 64) ** -0.5, 0.75, ((0, 8), (1, 4)))
    w_router = normal_values(keys[12], (D, EXPERTS), (4 * D) ** -0.5, 0.0625, ((0, 8),))
    w_gate = normal_values(keys[13], (EXPERTS, FF, D), D ** -0.5, 0.125, ((0, 8), (1, 4)))
    w_up = normal_values(keys[14], (EXPERTS, FF, D), D ** -0.5, 0.125, ((0, 8), (1, 4)))
    w_down = normal_values(keys[15], (EXPERTS, FF, D), (FF // 32) ** -0.5, 1.25, ((0, 8), (1, 4)))
    grad_out = normal_values(keys[16], (MICRO, SEQS, SEQ, D), 1.0, 6.0, ((1, 2), (2, 4)))
    return dict(hidden_in=hidden_in, segment_ids=segment_ids, expert_ids=expert_ids, capacity=capacity, norm_attn=norm_attn, norm_ffn=norm_ffn, norm_query=norm_query, norm_key=norm_key, w_query=w_query, w_key=w_key, w_value=w_value, w_out=w_out, w_router=w_router, w_gate=w_gate, w_up=w_up, w_down=w_down, grad_out=grad_out)


highest = lax.Precision.HIGHEST

@jax.custom_vjp
def low(v):
    return lax.optimization_barrier(v.astype(jnp.bfloat16)).astype(jnp.float32)

@jax.custom_vjp
def low_back(v):
    return v

def low_keep(v):
    return (low(v), None)

def low_pass(kept, grad):
    return (grad,)

def back_keep(v):
    return (v, None)

def back_low(kept, grad):
    return (low(grad),)
low.defvjp(low_keep, low_pass)
low_back.defvjp(back_keep, back_low)

def norm_rows(values, gain_vec):
    return values * lax.rsqrt(lax.optimization_barrier(jnp.mean(values * values, axis=-1, keepdims=True)) + 1e-06) * gain_vec

def rotate(values, cosine_table, sine_table):
    middle = values.shape[-1] // 2
    turned = jnp.concatenate([-values[..., middle:], values[..., :middle]], axis=-1)
    return values * cosine_table + turned * sine_table

def angles(positions, head_width):
    middle = head_width // 2
    frequency = jnp.power(1000000.0, -(2.0 * jnp.arange(middle, dtype=jnp.float32)) / head_width)
    phases = positions.astype(jnp.float32)[:, None] * frequency[None, :]
    phases = jnp.concatenate([phases, phases], axis=-1)
    return (jnp.cos(phases), jnp.sin(phases))

def attend(queries, key_heads, value_heads, segments):
    scores = jnp.einsum('qgd,kd->gqk', queries, key_heads, precision=highest) * queries.shape[-1] ** (-0.5)
    scores = low_back(scores)
    places = jnp.arange(queries.shape[0])
    allowed = (segments[:, None] == segments[None, :]) & (places[None, :] <= places[:, None])
    scores = jnp.where(allowed[None], scores, -1e+30)
    weights = low(jax.nn.softmax(scores, axis=-1))
    return jnp.einsum('gqk,kd->qgd', weights, value_heads, precision=highest)

def experts(rows_in, choices_ids, gate_weights, capacity, w_gate, w_up, w_down):
    row_count = rows_in.shape[0]
    expert_count = w_gate.shape[0]
    chosen = (choices_ids[:, :, None] == jnp.arange(expert_count)[None, None, :]).astype(jnp.int32)
    per_token = lax.optimization_barrier(jnp.sum(chosen, axis=1)).astype(jnp.int32)
    before = (jnp.cumsum(per_token, axis=0) - per_token).astype(jnp.int32)
    pair_ranks = lax.optimization_barrier(jnp.sum(chosen * before[:, None, :], axis=-1)).astype(jnp.int32)
    kept_pairs = pair_ranks < capacity[choices_ids]
    slot_index = jnp.where(kept_pairs, choices_ids * CAP + pair_ranks, expert_count * CAP).astype(jnp.int32).reshape(-1)
    token_index = jnp.repeat(jnp.arange(row_count, dtype=jnp.int32), choices_ids.shape[1])
    owners = jnp.zeros((expert_count * CAP + 1,), jnp.int32).at[slot_index].set(token_index)
    filled = jnp.zeros((expert_count * CAP + 1,), jnp.float32).at[slot_index].set(1.0)
    inputs = rows_in[owners[:expert_count * CAP]] * filled[:expert_count * CAP, None]
    inputs = inputs.reshape(expert_count, CAP, rows_in.shape[1])
    piece_width = w_gate.shape[1] // N_TENSOR
    produced = jnp.zeros((expert_count * CAP, rows_in.shape[1]), jnp.float32)
    for part_index in range(N_TENSOR):
        lowest = part_index * piece_width
        entering = low_back(inputs)
        gate_pre = low_back(jnp.einsum('ecd,efd->ecf', entering, w_gate[:, lowest:lowest + piece_width, :], precision=highest))
        upper_pre = low_back(jnp.einsum('ecd,efd->ecf', entering, w_up[:, lowest:lowest + piece_width, :], precision=highest))
        hidden = low(jax.nn.silu(gate_pre) * upper_pre)
        down_out = low(low_back(jnp.einsum('ecf,efd->ecd', hidden, w_down[:, lowest:lowest + piece_width, :], precision=highest)))
        produced = produced + down_out.reshape(expert_count * CAP, rows_in.shape[1])
    padded = jnp.concatenate([produced, jnp.zeros((1, rows_in.shape[1]), jnp.float32)], axis=0)
    pair_out = padded[slot_index].reshape(row_count, choices_ids.shape[1], rows_in.shape[1])
    return lax.optimization_barrier(jnp.sum(gate_weights[:, :, None] * pair_out, axis=1))

def layer_block(tokens, segments, choices_ids, capacity, weights):
    norm_attn, norm_ffn, norm_query, norm_key, w_query, w_key, w_value, w_out, w_router, w_gate, w_up, w_down = weights
    seq_count, length, breadth = tokens.shape
    head_count = w_query.shape[1] // HD
    kv_heads = w_key.shape[1] // HD
    group_size = head_count // kv_heads
    act_one = low(norm_rows(tokens, norm_attn))
    query_raw = low_back(jnp.einsum('bsd,dh->bsh', act_one, w_query, precision=highest))
    key_raw = low_back(jnp.einsum('bsd,dh->bsh', act_one, w_key, precision=highest))
    value_raw = low_back(jnp.einsum('bsd,dh->bsh', act_one, w_value, precision=highest))
    cosine_table, sine_table = angles(jnp.arange(length), HD)
    cosine_table = cosine_table[:, None, :]
    sine_table = sine_table[:, None, :]
    queries = low(rotate(norm_rows(query_raw.reshape(seq_count, length, head_count, HD), norm_query), cosine_table, sine_table))
    key_heads = low(rotate(norm_rows(key_raw.reshape(seq_count, length, kv_heads, HD), norm_key), cosine_table, sine_table))
    value_heads = low(value_raw.reshape(seq_count, length, kv_heads, HD))
    grouped = queries.reshape(seq_count, length, kv_heads, group_size, HD).transpose(0, 2, 1, 3, 4)
    grouped = grouped.reshape(seq_count * kv_heads, length, group_size, HD)
    key_rows = key_heads.transpose(0, 2, 1, 3).reshape(seq_count * kv_heads, length, HD)
    value_rows = value_heads.transpose(0, 2, 1, 3).reshape(seq_count * kv_heads, length, HD)
    segment_rows = jnp.repeat(segments, kv_heads, axis=0)
    checked = jax.checkpoint(attend)
    mixed = lax.map(lambda block_items: checked(block_items[0], block_items[1], block_items[2], block_items[3]), (grouped, key_rows, value_rows, segment_rows))
    mixed = mixed.reshape(seq_count, kv_heads, length, group_size, HD).transpose(0, 2, 1, 3, 4)
    mixed = low(low_back(mixed.reshape(seq_count, length, head_count * HD)))
    middle = tokens + low_back(jnp.einsum('bsh,dh->bsd', mixed, w_out, precision=highest))
    act_two = low(norm_rows(middle, norm_ffn))
    logits = low_back(jnp.einsum('bsd,de->bse', act_two, w_router, precision=highest))
    softmax_out = jax.nn.softmax(logits, axis=-1)
    picked = jnp.take_along_axis(softmax_out, choices_ids, axis=-1)
    gate_weights = picked / lax.optimization_barrier(jnp.sum(picked, axis=-1, keepdims=True))
    mixture = experts(act_two.reshape(seq_count * length, breadth), choices_ids.reshape(seq_count * length, -1), gate_weights.reshape(seq_count * length, -1), capacity, w_gate, w_up, w_down)
    return middle + low_back(mixture.reshape(seq_count, length, breadth))

def reference(hidden_in, segment_ids, expert_ids, capacity, norm_attn, norm_ffn, norm_query, norm_key, w_query, w_key, w_value, w_out, w_router, w_gate, w_up, w_down, grad_out):
    layer_params = (norm_attn, norm_ffn, norm_query, norm_key, w_query.astype(jnp.float32), w_key.astype(jnp.float32), w_value.astype(jnp.float32), w_out.astype(jnp.float32), w_router.astype(jnp.float32), w_gate.astype(jnp.float32), w_up.astype(jnp.float32), w_down.astype(jnp.float32))
    tokens = hidden_in.astype(jnp.float32)

    def whole_layer(inputs, weights):
        outputs = []
        for micro_index in range(MICRO):
            outputs.append(layer_block(inputs[micro_index], segment_ids[micro_index], expert_ids[micro_index], capacity, weights))
        return jnp.stack(outputs)
    result, pullback = jax.vjp(whole_layer, tokens, layer_params)
    grad_tokens, gradients = pullback(grad_out.astype(jnp.float32))
    return (result, grad_tokens, gradients[0], gradients[1], gradients[2], gradients[3], gradients[4], gradients[5], gradients[6], gradients[7], gradients[8], gradients[9], gradients[10], gradients[11])
```

```python
import jax
import jax.numpy as jnp
from jax import lax
from jax.sharding import PartitionSpec as P

B, C, T = "batch", "ctx", "tensor"
BC = (B, C)
ALL = (B, C, T)
f32 = jnp.float32
bf16 = jnp.bfloat16
EPS = 1e-06


def dot(a, b, ca, cb):
    return lax.dot_general(a, b, (((ca,), (cb,)), ((), ())), preferred_element_type=f32)


def nn(a, b):
    return dot(a, b, 1, 0)


def nt(a, b):
    return dot(a, b, 1, 1)


def tn(a, b):
    return dot(a, b, 0, 0)


def bdot(a, b, ca, cb):
    return lax.dot_general(a, b, (((ca,), (cb,)), ((0,), (0,))), preferred_element_type=f32)


def pad_cols(v, width):
    return jnp.pad(v, ((0, 0), (0, width - v.shape[1])))


def inv_rms(v):
    return lax.rsqrt(jnp.mean(v * v, axis=-1, keepdims=True) + EPS)


def turn(v):
    half = v.shape[-1] // 2
    return jnp.concatenate([-v[..., half:], v[..., :half]], axis=-1)


def angles(positions, width):
    half = width // 2
    frequency = jnp.power(1000000.0, -(2.0 * jnp.arange(half, dtype=f32)) / width)
    phases = positions.astype(f32)[:, None] * frequency[None, :]
    phases = jnp.concatenate([phases, phases], axis=-1)
    return jnp.cos(phases), jnp.sin(phases)


def norm_back(v, r, gain, grad):
    scaled = gain * grad
    grad_v = r * scaled - v * (r * r * r) * jnp.mean(v * scaled, axis=-1, keepdims=True)
    return grad_v, grad * v * r


def heads_forward(raw, gain, cosine, sine):
    v = raw * inv_rms(raw) * gain
    return (v * cosine + turn(v) * sine).astype(bf16)


def heads_back(raw, gain, cosine, sine, grad):
    grad = grad * cosine - turn(grad) * sine
    return norm_back(raw, inv_rms(raw), gain, grad)


def gather_t(v):
    count = lax.axis_size(T)
    return lax.all_to_all(jnp.concatenate([v] * count, axis=0), T, 0, 0, tiled=True)


def sum_t(v):
    count = lax.axis_size(T)
    got = lax.all_to_all(v.astype(bf16), T, 0, 0, tiled=True)
    got = got.reshape(count, v.shape[0] // count, v.shape[1])
    return jnp.sum(got.astype(f32), axis=0)


def sum_all(v):
    width = v.shape[1]
    halves = v.reshape(2, -1, width)
    me = lax.axis_index(B)
    other = lax.ppermute(lax.dynamic_index_in_dim(halves, 1 - me, 0, False), B, [(0, 1), (1, 0)])
    own = lax.dynamic_index_in_dim(halves, me, 0, False)
    chip = (own.astype(f32) + other.astype(f32)).astype(bf16)
    plane = sum_t(chip).astype(bf16)
    count = lax.axis_size(C)
    got = lax.all_to_all(plane, C, 0, 0, tiled=True)
    got = got.reshape(count, plane.shape[0] // count, width)
    return jnp.sum(got.astype(f32), axis=0)


def to_features(v):
    return lax.all_to_all(v, BC, 1, 0, tiled=True)


def body(
    hidden_in,
    segment_ids,
    expert_ids,
    capacity,
    norm_attn,
    norm_ffn,
    norm_query,
    norm_key,
    w_query,
    w_key,
    w_value,
    w_out,
    w_router,
    w_gate,
    w_up,
    w_down,
    grad_out,
):
    micro, _, span, width = hidden_in.shape
    rows = micro * span
    hd = norm_query.shape[0]
    topk = expert_ids.shape[3]
    experts = w_router.shape[1]
    mine = w_gate.shape[0]
    nb, nc, nt_ = lax.axis_size(B), lax.axis_size(C), lax.axis_size(T)
    sources = nb * nc
    cut = rows // nt_
    b, c, t = lax.axis_index(B), lax.axis_index(C), lax.axis_index(T)
    place = b * nc + c
    seq = span * nc
    back = (seq // 2 - 1 + span - 1) // span
    heads = w_query.shape[1] // hd
    q_cols = heads * hd
    scale = hd ** (-0.5)
    routed = -(-experts // 128) * 128

    x = hidden_in.reshape(rows, width)
    dy = grad_out.reshape(rows, width)

    w_qkv = lax.all_gather(
        jnp.concatenate([w_query, w_key, w_value], axis=1), BC, axis=0, tiled=True
    )
    w_or = lax.all_gather(
        jnp.concatenate([w_out, pad_cols(w_router, routed)], axis=1), BC, axis=0, tiled=True
    )
    out_w = w_or[:, :q_cols]
    router_w = w_or[:, q_cols : q_cols + experts]

    ids_own = expert_ids.reshape(rows, topk).T
    info = jnp.concatenate([ids_own, segment_ids.reshape(1, rows)], axis=0)
    info = jnp.pad(info, ((0, -(-(topk + 1) // 8) * 8 - topk - 1), (0, 0)))
    tall = info.shape[0]
    info = lax.all_to_all(jnp.concatenate([info] * sources, axis=0), BC, 0, 0, tiled=True)
    info = info.reshape(sources, tall, rows)
    ids_all = info[:, :topk]
    seg_all = info[:, topk].reshape(nb, nc, micro, span)
    local = place * mine + jnp.arange(mine)
    hot = jnp.sum((ids_all[:, :, None, :] == local[None, None, :, None]).astype(f32), axis=1)
    hot = hot.reshape(sources, mine, micro, span)
    upper = (jnp.arange(span)[:, None] < jnp.arange(span)[None, :]).astype(bf16)
    within = nn(hot.astype(bf16).reshape(-1, span), upper).reshape(hot.shape)
    totals = jnp.sum(hot, axis=-1)
    earlier = jnp.arange(sources)[:, None] < jnp.arange(sources)[None, :]
    before = jnp.sum(jnp.where(earlier[:, :, None, None], totals[:, None], 0.0), axis=0)
    rank = within + before[..., None]
    room = lax.dynamic_slice(capacity, (place * mine,), (mine,)).astype(f32)
    kept = jnp.where(rank < room[None, :, None, None], hot, 0.0)
    kept = kept.reshape(nb, nc, mine, nt_, cut).transpose(0, 3, 1, 4, 2).reshape(-1, mine)
    ids_rows = ids_all.reshape(nb, nc, topk, nt_, cut).transpose(0, 3, 1, 4, 2).reshape(-1, topk)
    names = jnp.arange(experts)
    chosen_all = jnp.sum((ids_rows[:, :, None] == names).astype(f32), axis=1)
    ids_slice = lax.dynamic_slice(expert_ids.reshape(rows, topk), (t * cut, 0), (cut, topk))
    chosen = jnp.sum((ids_slice[:, :, None] == names).astype(f32), axis=1)

    xf = x.astype(f32)
    act1 = (xf * inv_rms(xf) * norm_attn).astype(bf16)
    act1_cols = to_features(act1)
    dy_slice = lax.dynamic_slice(dy, (t * cut, 0), (cut, width))
    dy_all = lax.all_gather(dy_slice, (B, T, C), axis=0, tiled=True)
    qkv = nn(act1, w_qkv)
    positions = c * span + jnp.arange(span)
    cosine, sine = angles(positions, hd)
    cosine = jnp.concatenate([cosine] * micro, axis=0)
    sine = jnp.concatenate([sine] * micro, axis=0)
    q_raw = qkv[:, :q_cols].reshape(rows, heads, hd)
    k_raw = qkv[:, q_cols : q_cols + hd]
    q = heads_forward(q_raw, norm_query, cosine[:, None], sine[:, None])
    k = heads_forward(k_raw, norm_key, cosine, sine)
    kv = jnp.concatenate([k, qkv[:, q_cols + hd :].astype(bf16)], axis=1)
    blocks = [
        lax.ppermute(kv, C, [(i, i + s) for i in range(nc - s)]) for s in range(back, 0, -1)
    ]
    window = jnp.stack(blocks + [kv]).reshape(back + 1, micro, span, 2 * hd)
    window = window.transpose(1, 0, 2, 3).reshape(micro, (back + 1) * span, 2 * hd)
    keys, values = window[..., :hd], window[..., hd:]
    seg_seq = lax.dynamic_index_in_dim(seg_all, b, 0, False)
    seg_seq = jnp.pad(seg_seq, ((back, 0), (0, 0), (0, 0)), constant_values=-1)
    seg_win = lax.dynamic_slice(seg_seq, (c, 0, 0), (back + 1, micro, span))
    seg_win = seg_win.transpose(1, 0, 2).reshape(micro, -1)
    seg_own = segment_ids.reshape(micro, span)
    allowed = (seg_own[:, :, None] == seg_win[:, None, :]) & (
        jnp.arange((back + 1) * span)[None, None, :] <= back * span + jnp.arange(span)[None, :, None]
    )
    qg = q.reshape(micro, span, heads, hd).transpose(0, 2, 1, 3)
    qg = qg.reshape(micro, heads * span, hd)
    scores = bdot(qg, keys, 2, 2).reshape(micro, heads, span, -1) * scale
    scores = jnp.where(allowed[:, None], scores, -1e30)
    top = jnp.max(scores, axis=-1, keepdims=True)
    weight = jnp.exp(scores - top)
    total = jnp.sum(weight, axis=-1, keepdims=True)
    probs = weight / total
    log_total = top + jnp.log(total)
    probs_low = probs.astype(bf16).reshape(micro, heads * span, -1)
    mixed = bdot(probs_low, values, 2, 1).astype(bf16).reshape(micro, heads, span, hd)
    mixed = mixed.transpose(0, 2, 1, 3).reshape(rows, q_cols)
    branch = sum_t(nt(mixed, out_w))
    x_slice = lax.dynamic_slice(x, (t * cut, 0), (cut, width)).astype(f32)
    middle = x_slice + branch
    r2 = inv_rms(middle)
    act2 = (middle * r2 * norm_ffn).astype(bf16)
    act2_all = lax.all_gather(act2, (B, T, C), axis=0, tiled=True)
    mixed_later, act2_all = lax.optimization_barrier((mixed, act2_all))
    mixed_all = lax.all_gather(mixed_later, BC, axis=0, tiled=True)

    logits_all = nn(act2_all, router_w)
    shifted = jnp.exp(logits_all - jnp.max(logits_all, axis=-1, keepdims=True)) * chosen_all
    gates_all = shifted / jnp.sum(shifted, axis=-1, keepdims=True)
    gates = lax.dynamic_slice(gates_all, (0, place * mine), (gates_all.shape[0], mine)) * kept
    hidden = mine * w_gate.shape[1]
    gate_w = w_gate.reshape(hidden, width)
    up_w = w_up.reshape(hidden, width)
    down_w = w_down.reshape(hidden, width)
    owner = jnp.arange(hidden)[None, :] // w_gate.shape[1]

    def spread(v):
        wide = jnp.where(owner == 0, v[:, 0:1], 0.0)
        for e in range(1, mine):
            wide = jnp.where(owner == e, v[:, e : e + 1], wide)
        return wide

    dy_down = nt(dy_all, down_w)
    gate_pre = nt(act2_all, gate_w)
    up_pre = nt(act2_all, up_w)
    sig = jax.nn.sigmoid(gate_pre)
    silu = gate_pre * sig
    gates_wide = spread(gates)
    hid = silu * up_pre
    hid_gated = (gates_wide * hid).astype(bf16)
    agree = hid * dy_down
    d_gates = jnp.stack(
        [jnp.sum(jnp.where(owner == e, agree, 0.0), axis=1) for e in range(mine)], axis=1
    )
    d_gates = jnp.where(kept > 0.0, d_gates, 0.0)
    d_hid = gates_wide * dy_down
    d_gate = (d_hid * up_pre * sig * (1.0 + gate_pre * (1.0 - sig))).astype(bf16)
    d_up = (d_hid * silu).astype(bf16)
    d_in = (nn(d_gate, gate_w) + nn(d_up, up_w)).astype(bf16)
    d_gates_wide = lax.dynamic_update_slice(
        jnp.zeros((d_in.shape[0], routed), bf16), d_gates.astype(bf16), (0, place * mine)
    )
    d_in_sum = sum_all(jnp.concatenate([d_in, d_gates_wide], axis=1))
    out_part = nn(hid_gated, down_w).astype(bf16)
    grad_down = tn(hid_gated, dy_all).reshape(w_down.shape)
    grad_gate = tn(d_gate, act2_all).reshape(w_gate.shape)
    grad_up = tn(d_up, act2_all).reshape(w_up.shape)

    d_gates_slice = d_in_sum[:, width : width + experts]
    logits = nn(act2, router_w)
    probs_r = jax.nn.softmax(logits, axis=-1)
    picked = probs_r * chosen
    picked_sum = jnp.sum(picked, axis=-1, keepdims=True)
    gates_slice = picked / picked_sum
    lean = jnp.sum(d_gates_slice * gates_slice, axis=-1, keepdims=True)
    c_grad = chosen * (d_gates_slice - lean) / picked_sum
    d_logits = probs_r * (c_grad - jnp.sum(probs_r * c_grad, axis=-1, keepdims=True))
    d_logits = d_logits.astype(bf16)
    d_act2 = d_in_sum[:, :width] + nt(d_logits, router_w)
    d_norm, gain_rows = norm_back(middle, r2, norm_ffn, d_act2)
    gain_ffn = jnp.sum(gain_rows, axis=0)
    dy_f = dy_slice.astype(f32)
    d_middle = dy_f + d_norm
    packed = jnp.concatenate([d_middle.astype(bf16), pad_cols(d_logits, routed)], axis=1)
    packed = gather_t(packed)
    d_branch = packed[:, :width]
    d_logits_rows = packed[:, width:]

    d_mixed = nn(d_branch, out_w).astype(bf16)
    d_branch_cols = to_features(d_branch)
    grad_out_w = tn(d_branch_cols, mixed_all)
    dmg = d_mixed.reshape(micro, span, heads, hd).transpose(0, 2, 1, 3)
    dmg = dmg.reshape(micro, heads * span, hd)
    again = bdot(qg, keys, 2, 2).reshape(micro, heads, span, -1) * scale
    probs2 = jnp.where(allowed[:, None], jnp.exp(again - log_total), 0.0)
    d_probs = bdot(dmg, values, 2, 2).reshape(probs2.shape)
    row_dot = jnp.sum(probs2 * d_probs, axis=-1, keepdims=True)
    d_scores = (probs2 * (d_probs - row_dot)).astype(bf16).reshape(micro, heads * span, -1)
    d_q = bdot(d_scores, keys, 2, 1) * scale
    d_keys = bdot(d_scores, qg, 1, 1) * scale
    d_values = bdot(probs2.astype(bf16).reshape(d_scores.shape), dmg, 1, 1)
    d_kv = jnp.concatenate([d_keys, d_values], axis=-1).reshape(micro, back + 1, span, 2 * hd)
    d_kv_own = d_kv[:, back].reshape(rows, 2 * hd)
    for s in range(1, back + 1):
        piece = d_kv[:, back - s].reshape(rows, 2 * hd).astype(bf16)
        d_kv_own = d_kv_own + lax.ppermute(piece, C, [(i + s, i) for i in range(nc - s)]).astype(f32)
    d_q = d_q.reshape(micro, heads, span, hd).transpose(0, 2, 1, 3).reshape(rows, heads, hd)
    d_q_raw, gain_q_rows = heads_back(q_raw, norm_query, cosine[:, None], sine[:, None], d_q)
    d_k_raw, gain_k_rows = heads_back(k_raw, norm_key, cosine, sine, d_kv_own[:, :hd])
    gain_q = jnp.sum(gain_q_rows, axis=(0, 1))
    gain_k = jnp.sum(gain_k_rows, axis=0)
    d_qkv = jnp.concatenate([d_q_raw.reshape(rows, q_cols), d_k_raw, d_kv_own[:, hd:]], axis=1)
    d_qkv = d_qkv.astype(bf16)
    late = lax.all_gather(jnp.concatenate([d_qkv, d_logits_rows], axis=1), BC, axis=0, tiled=True)
    d_act1 = sum_t(nt(d_qkv, w_qkv))
    d_norm1, gain1_rows = norm_back(x_slice, inv_rms(x_slice), norm_attn, d_act1)
    gain_attn = jnp.sum(gain1_rows, axis=0)
    grad_in = gather_t((d_norm + d_norm1).astype(bf16)).astype(f32) + dy.astype(f32)

    grad_qkv = tn(act1_cols, late[:, : d_qkv.shape[1]])
    d_logits_all = late[:, d_qkv.shape[1] : d_qkv.shape[1] + experts]
    d_logits_all = d_logits_all.reshape(nb, nc, nt_, cut, experts).transpose(0, 2, 1, 3, 4)
    d_logits_all = d_logits_all.reshape(-1, experts)
    own_cols = width // sources
    act2_cols = lax.dynamic_slice(act2_all, (0, place * own_cols), (act2_all.shape[0], own_cols))
    grad_router = tn(act2_cols, d_logits_all)

    pieces = [v.reshape(sources, -1) for v in (gain_attn, gain_ffn, gain_q, gain_k)]
    sizes = [v.shape[1] for v in pieces]
    flat = jnp.concatenate(pieces, axis=1)
    lanes = -(-flat.shape[1] // 128) * 128
    flat = jnp.broadcast_to(pad_cols(flat, lanes)[:, None], (sources, nt_, lanes))
    flat = lax.all_to_all(flat.reshape(-1, lanes), ALL, 0, 0, tiled=True)
    flat = jnp.sum(flat, axis=0)
    gains, start = [], 0
    for size in sizes:
        gains.append(flat[start : start + size])
        start += size

    hidden_out = gather_t((branch + sum_all(out_part)).astype(bf16)).astype(f32) + xf
    shape = hidden_in.shape
    return (
        hidden_out.reshape(shape),
        grad_in.reshape(shape),
        gains[0],
        gains[1],
        gains[2],
        gains[3],
        grad_qkv[:, :q_cols],
        grad_qkv[:, q_cols : q_cols + hd],
        grad_qkv[:, q_cols + hd :],
        grad_out_w,
        grad_router,
        grad_gate,
        grad_up,
        grad_down,
    )


def solution(mesh):
    rows = P(None, B, C, None)
    ids = P(None, B, C)
    whole = P()
    matrix = P(BC, T)
    router = P(BC, None)
    expert = P(BC, T, None)
    vector = P(BC)
    in_specs = (rows, ids, rows) + (whole,) * 5 + (matrix,) * 4 + (router,) + (expert,) * 3 + (rows,)
    out_specs = (rows, rows) + (vector,) * 4 + (matrix,) * 4 + (router,) + (expert,) * 3
    return jax.shard_map(body, mesh=mesh, in_specs=in_specs, out_specs=out_specs, check_vma=False)
```

```python
import functools

import jax
import jax.numpy as jnp
from jax import lax
from jax.experimental import pallas as pl
from jax.experimental.pallas import tpu as pltpu
from jax.sharding import PartitionSpec as P

B, C, T = "batch", "ctx", "tensor"
BC = (B, C)
ALL = (B, C, T)
f32 = jnp.float32
bf16 = jnp.bfloat16
EPS = 1e-06


def dot(a, b, ca, cb):
    return lax.dot_general(a, b, (((ca,), (cb,)), ((), ())), preferred_element_type=f32)


def nn(a, b):
    return dot(a, b, 1, 0)


def nt(a, b):
    return dot(a, b, 1, 1)


def tn(a, b):
    return dot(a, b, 0, 0)


def bdot(a, b, ca, cb):
    return lax.dot_general(a, b, (((ca,), (cb,)), ((0,), (0,))), preferred_element_type=f32)


def after(*values):
    return lax.optimization_barrier(values)


def pad_cols(v, width):
    return jnp.pad(v, ((0, 0), (0, width - v.shape[1])))


def inv_rms(v):
    return lax.rsqrt(jnp.mean(v * v, axis=-1, keepdims=True) + EPS)


def turn(v):
    half = v.shape[-1] // 2
    return jnp.concatenate([-v[..., half:], v[..., :half]], axis=-1)


def angles(positions, width):
    half = width // 2
    frequency = jnp.power(1000000.0, -(2.0 * jnp.arange(half, dtype=f32)) / width)
    phases = positions.astype(f32)[:, None] * frequency[None, :]
    phases = jnp.concatenate([phases, phases], axis=-1)
    return jnp.cos(phases), jnp.sin(phases)


def norm_back(v, r, gain, grad):
    scaled = gain * grad
    grad_v = r * scaled - v * (r * r * r) * jnp.mean(v * scaled, axis=-1, keepdims=True)
    return grad_v, grad * v * r


def heads_forward(raw, gain, cosine, sine):
    v = raw * inv_rms(raw) * gain
    return (v * cosine + turn(v) * sine).astype(bf16)


def heads_back(raw, gain, cosine, sine, grad):
    grad = grad * cosine - turn(grad) * sine
    return norm_back(raw, inv_rms(raw), gain, grad)


def gather_t(v):
    count = lax.axis_size(T)
    return lax.all_to_all(jnp.concatenate([v] * count, axis=0), T, 0, 0, tiled=True)


def sum_t(v):
    count = lax.axis_size(T)
    got = lax.all_to_all(v.astype(bf16), T, 0, 0, tiled=True)
    got = got.reshape(count, v.shape[0] // count, v.shape[1])
    return jnp.sum(got.astype(f32), axis=0)


def swap(v):
    return lax.ppermute(v, B, [(0, 1), (1, 0)])


def across(v, k):
    return lax.ppermute(v, T, [(i, i ^ k) for i in range(lax.axis_size(T))])


def add_low(*parts):
    total = parts[0].astype(f32)
    for part in parts[1:]:
        total = total + part.astype(f32)
    return total.astype(bf16)


def gather_c(v):
    count = lax.axis_size(C)
    return lax.all_to_all(jnp.concatenate([v] * count, axis=0), C, 0, 0, tiled=True)


def spread_plane(own):
    half = own.shape[0] // 2
    from_x, from_y = across(own, 1), across(own, 2)
    low, high = across(from_x[:half], 2), across(from_y[half:], 1)
    return [own, from_x, from_y, jnp.concatenate([low, high], axis=0)]


def sum_plane(own, ring, corner, held=()):
    diagonal = add_low(corner[0][0], swap(corner[1])[0])
    half = diagonal.shape[0] // 2
    from_x, from_y = across(diagonal[:half], 1), across(diagonal[half:], 2)
    ring_far = swap(ring[1])
    own_far = swap(own[1])
    from_x, from_y, *held = after(from_x, from_y, *held)
    east = add_low(ring[0][0], ring_far[0])
    north = add_low(ring[0][1], ring_far[1])
    east = jnp.concatenate([east[:half], add_low(east[half:], from_y)], axis=0)
    north = jnp.concatenate([add_low(north[:half], from_x), north[half:]], axis=0)
    return add_low(own[0][0], own_far[0], across(east, 1), across(north, 2)), held


def to_features(v):
    return lax.all_to_all(v, BC, 1, 0, tiled=True)


def send_c(plane):
    count = lax.axis_size(C)
    got = lax.all_to_all(plane, C, 0, 0, tiled=True)
    return got.reshape(count, plane.shape[0] // count, plane.shape[1])


SLAB = 256


def sum_c_permute(plane):
    count = lax.axis_size(C)
    cut = plane.shape[0] // count
    c = lax.axis_index(C)
    block = lambda k: lax.dynamic_slice(plane, (((c + k) % count) * cut, 0), (cut, plane.shape[1]))
    total = block(0).astype(f32)
    for k in range(1, count):
        got = lax.ppermute(block(k), C, [(i, (i + k) % count) for i in range(count)])
        total = total + got.astype(f32)
    return total


def expert_kernel(count, first, where_ref, *refs):
    acts, dys, marks = refs[:count], refs[count : count + 2], refs[count + 2 : 2 * count + 2]
    router_ref, place_ref = refs[2 * count + 2 : 2 * count + 4]
    weights_hbm = refs[2 * count + 4 : 2 * count + 7]
    tail = refs[-20:]
    act_all, dy_all, hid_all, dg_all, du_all, near, far = tail[:7]
    act_b, dy_b, hid_b, dg_b, du_b, din_b, mark_b = tail[7:14]
    gate_w, up_w, down_w = tail[14:17]
    in_sem, w_sem, out_sem = tail[17:]
    i = pl.program_id(0)
    width = act_b.shape[2]
    hidden = gate_w.shape[0]
    src = pl.ds(pl.multiple_of(i * SLAB, SLAB), SLAB)
    base = first + i * count * SLAB
    stored = ((act_b, act_all), (dy_b, dy_all), (hid_b, hid_all), (dg_b, dg_all), (du_b, du_all))
    weights = [
        pltpu.make_async_copy(v, w, w_sem.at[k])
        for k, (v, w) in enumerate(zip(weights_hbm, (gate_w, up_w, down_w)))
    ]

    piece = pl.num_programs(0) * SLAB

    def load(k, p):
        if k == 0:
            return pltpu.make_async_copy(acts[p].at[src], act_b.at[p], in_sem.at[0, p])
        rows = pl.ds(pl.multiple_of(where_ref[count + p] * piece + i * SLAB, SLAB), SLAB)
        return pltpu.make_async_copy(dys[p // (count // 2)].at[rows], dy_b.at[p], in_sem.at[1, p])

    def stores(p):
        rows = pl.ds(pl.multiple_of(base + p * SLAB, SLAB), SLAB)
        return [
            pltpu.make_async_copy(v.at[p], to.at[rows], out_sem.at[k, p])
            for k, (v, to) in enumerate(stored)
        ]

    def give(p, place, to):
        return pltpu.make_async_copy(din_b.at[p], to.at[place, src], out_sem.at[5, p])

    load(0, 0).start()

    @pl.when(i == 0)
    def _():
        weights[0].start()
        weights[1].start()

    load(1, 0).start()

    @pl.when(i == 0)
    def _():
        weights[2].start()

    for p in range(1, count):
        load(0, p).start()
        load(1, p).start()
    for p in range(count):
        mark_b[p] = marks[p][0]

    @pl.when(i == 0)
    def _():
        weights[0].wait()
        weights[1].wait()

    def one(p, carry):
        for k, buffer in enumerate((act_b, dy_b)):
            pltpu.make_async_copy(acts[0].at[src], buffer.at[p], in_sem.at[k, p]).wait()
        act = act_b[p]
        mark = mark_b[p]
        logits = nn(act, router_ref[...])
        top = jnp.max(jnp.where(mark > 0.5, logits, -1e30), axis=1, keepdims=True)
        parts = jnp.where(mark > 0.5, jnp.exp(logits - top), 0.0)
        parts = parts / jnp.sum(parts, axis=1, keepdims=True)
        gates = jnp.where(mark > 1.5, parts, 0.0)
        high = gates.astype(bf16)
        low = (gates - high.astype(f32)).astype(bf16)

        @pl.when((p == 0) & (i == 0))
        def _():
            weights[2].wait()

        place = place_ref[...]
        wide = nn(high, place) + nn(low, place)
        gate = nt(act, gate_w[...])
        up = nt(act, up_w[...])
        dyw = nt(dy_b[p], down_w[...])
        sig = 0.5 * jnp.tanh(0.5 * gate) + 0.5
        silu = gate * sig
        hid = silu * up
        hid_b[p] = (wide * hid).astype(bf16)
        share = nt((hid * dyw).astype(bf16), place)
        d_hid = wide * dyw
        dg_b[p] = (d_hid * up * (sig + silu * (1.0 - sig))).astype(bf16)
        du_b[p] = (d_hid * silu).astype(bf16)
        din_b[p, :, width:] = jnp.where(mark > 1.5, share, 0.0).astype(bf16)
        for w in range(0, width, 512):
            cols = slice(w, w + 512)
            total = nn(dg_b[p], gate_w[:, cols]) + nn(du_b[p], up_w[:, cols])
            din_b[p, :, cols] = total.astype(bf16)
        for copy in stores(p):
            copy.start()

        @pl.when(p < count // 2)
        def _():
            give(p, p, near).start()

        @pl.when(p >= count // 2)
        def _():
            give(p, p - count // 2, far).start()

        return carry

    lax.fori_loop(0, count, one, 0)
    for p in range(count):
        for copy in stores(p):
            copy.wait()
        give(p, p % (count // 2), (near, far)[p // (count // 2)]).wait()


def expert_pieces(first, where, acts, dys, marks, consts, held, total_rows):
    count = len(acts)
    rows, width = acts[0].shape
    hidden = consts[2].shape[0]
    routed = consts[0].shape[1]
    left = pl.BlockSpec(memory_space=pl.ANY)
    in_specs = [left] * (count + 2)
    in_specs += [
        pl.BlockSpec((1, SLAB, routed), lambda i, w, p=p: (w[p], i, 0)) for p in range(count)
    ]
    in_specs += [
        pl.BlockSpec(v.shape, lambda i, w: (0, 0), pipeline_mode=pl.Buffered(1)) for v in consts[:2]
    ]
    in_specs += [left] * 3
    out_shape = [jax.ShapeDtypeStruct((total_rows, width), bf16)] * 2
    out_shape += [jax.ShapeDtypeStruct((total_rows, hidden), bf16)] * 3
    out_shape += [jax.ShapeDtypeStruct((count // 2, rows, width + routed), bf16)] * 2
    args = [where, *acts, *dys, *([marks] * count), *consts]
    aliases = {}
    if held is not None:
        for k, v in enumerate(held):
            aliases[len(args)] = k
            args.append(v)
            in_specs.append(left)
    outs = pl.pallas_call(
        functools.partial(expert_kernel, count, first),
        grid_spec=pltpu.PrefetchScalarGridSpec(
            num_scalar_prefetch=1,
            grid=(rows // SLAB,),
            in_specs=in_specs,
            out_specs=[left] * 7,
            scratch_shapes=[pltpu.VMEM((count, SLAB, width), bf16)] * 2
            + [pltpu.VMEM((count, SLAB, hidden), bf16)] * 3
            + [pltpu.VMEM((count, SLAB, width + routed), bf16)]
            + [pltpu.VMEM((count, SLAB, routed), f32)]
            + [pltpu.VMEM((hidden, width), bf16)] * 3
            + [pltpu.SemaphoreType.DMA((2, count))]
            + [pltpu.SemaphoreType.DMA((3,))]
            + [pltpu.SemaphoreType.DMA((6, count))],
        ),
        out_shape=out_shape,
        input_output_aliases=aliases,
        compiler_params=pltpu.CompilerParams(vmem_limit_bytes=56 << 20),
        cost_estimate=pl.CostEstimate(flops=1000, bytes_accessed=1000, transcendentals=0),
    )(*args)
    return outs[:5], outs[5:]


def attend_back_kernel(heads, scale, q_ref, raw_ref, kv_ref, bias_ref, dm_ref, cos_ref, sin_ref, gain_ref, dq_ref, dkv_ref, gq_ref, rows_q, rows_m, rows_p, rows_s):
    span = q_ref.shape[0]
    hd = gain_ref.shape[1]
    keys, values = kv_ref[0, :, :hd], kv_ref[0, :, hd:]
    bias = bias_ref[0]
    cosine, sine = cos_ref[...], sin_ref[...]
    gain = gain_ref[...]

    @pl.when(pl.program_id(0) == 0)
    def _():
        gq_ref[...] = jnp.zeros_like(gq_ref)

    total = jnp.zeros((1, hd), f32)
    for h in range(heads):
        cols = slice(h * hd, (h + 1) * hd)
        lines = slice(h * span, (h + 1) * span)
        q = q_ref[:, cols]
        dm = dm_ref[:, cols]
        rows_q[lines, :] = q
        rows_m[lines, :] = dm
        scores = nt(q, keys) * scale + bias
        weight = jnp.exp(scores - jnp.max(scores, axis=1, keepdims=True))
        probs = weight / jnp.sum(weight, axis=1, keepdims=True)
        d_probs = nt(dm, values)
        d_scores = probs * (d_probs - jnp.sum(probs * d_probs, axis=1, keepdims=True))
        low = d_scores.astype(bf16)
        rows_p[lines, :] = probs.astype(bf16)
        rows_s[lines, :] = low
        d_q = nn(low, keys) * scale
        grad = d_q * cosine - pltpu.roll(d_q, hd // 2, 1) * sine
        raw = raw_ref[:, cols]
        d_raw, gain_rows = norm_back(raw, inv_rms(raw), gain, grad)
        dq_ref[:, cols] = d_raw.astype(bf16)
        total = total + jnp.sum(gain_rows, axis=0, keepdims=True)
    gq_ref[...] += total
    dkv_ref[0, :, :hd] = (tn(rows_s[...], rows_q[...]) * scale).astype(bf16)
    dkv_ref[0, :, hd:] = tn(rows_p[...], rows_m[...]).astype(bf16)


def attend_back(q, qkv, window, bias, d_mixed, cosine, sine, gain):
    micro, reach, pair = window.shape
    hd = pair // 2
    span, q_cols = q.shape[0] // micro, q.shape[1]
    heads = q_cols // hd
    row = lambda m: (m, 0)
    flat = lambda m: (0, 0)
    deep = lambda m: (m, 0, 0)
    return pl.pallas_call(
        functools.partial(attend_back_kernel, heads, hd ** (-0.5)),
        grid=(micro,),
        in_specs=[
            pl.BlockSpec((span, q_cols), row),
            pl.BlockSpec((span, q_cols), row),
            pl.BlockSpec((1, reach, pair), deep),
            pl.BlockSpec((1, span, reach), deep),
            pl.BlockSpec((span, q_cols), row),
            pl.BlockSpec((span, hd), flat),
            pl.BlockSpec((span, hd), flat),
            pl.BlockSpec((1, hd), flat),
        ],
        out_specs=[
            pl.BlockSpec((span, q_cols), row),
            pl.BlockSpec((1, reach, pair), deep),
            pl.BlockSpec((1, hd), flat),
        ],
        out_shape=[
            jax.ShapeDtypeStruct(q.shape, bf16),
            jax.ShapeDtypeStruct(window.shape, bf16),
            jax.ShapeDtypeStruct((1, hd), f32),
        ],
        scratch_shapes=[pltpu.VMEM((heads * span, hd), bf16)] * 2
        + [pltpu.VMEM((heads * span, reach), bf16)] * 2,
        compiler_params=pltpu.CompilerParams(vmem_limit_bytes=32 << 20),
        cost_estimate=pl.CostEstimate(
            flops=10 * micro * heads * span * reach * hd,
            bytes_accessed=10 * micro * span * q_cols,
            transcendentals=micro * heads * span * reach,
        ),
    )(q, qkv, window, bias, d_mixed, cosine, sine, gain)


def turn_back_kernel(experts, got_ref, act_ref, mid_ref, dy_ref, chosen_ref, router_ref, gain_ref, dn_ref, low_ref, dl_ref, gain_out):
    width = mid_ref.shape[1]
    total = got_ref[0].astype(f32)
    for k in range(1, got_ref.shape[0]):
        total = total + got_ref[k].astype(f32)
    d_gates = total[:, width:]
    router = router_ref[...]
    chosen = chosen_ref[...]
    logits = nn(act_ref[...], router)
    real = lax.broadcasted_iota(jnp.int32, logits.shape, 1) < experts
    logits = jnp.where(real, logits, -1e30)
    weight = jnp.exp(logits - jnp.max(logits, axis=1, keepdims=True))
    probs = weight / jnp.sum(weight, axis=1, keepdims=True)
    picked = probs * chosen
    picked_sum = jnp.sum(picked, axis=1, keepdims=True)
    lean = jnp.sum(d_gates * picked / picked_sum, axis=1, keepdims=True)
    c_grad = chosen * (d_gates - lean) / picked_sum
    d_logits = probs * (c_grad - jnp.sum(probs * c_grad, axis=1, keepdims=True))
    d_logits = jnp.where(real, d_logits, 0.0).astype(bf16)
    dl_ref[...] = d_logits
    d_act = total[:, :width] + nt(d_logits, router)
    middle = mid_ref[...]
    d_norm, gain_rows = norm_back(middle, inv_rms(middle), gain_ref[...], d_act)
    dn_ref[...] = d_norm
    low_ref[...] = (dy_ref[...].astype(f32) + d_norm).astype(bf16)
    gain_out[...] = jnp.sum(gain_rows, axis=0, keepdims=True)


def turn_back(experts, got, act2, middle, dy_slice, chosen, router, gain):
    cut, width = middle.shape
    routed = router.shape[1]
    return pl.pallas_call(
        functools.partial(turn_back_kernel, experts),
        out_shape=[
            jax.ShapeDtypeStruct((cut, width), f32),
            jax.ShapeDtypeStruct((cut, width), bf16),
            jax.ShapeDtypeStruct((cut, routed), bf16),
            jax.ShapeDtypeStruct((1, width), f32),
        ],
        compiler_params=pltpu.CompilerParams(vmem_limit_bytes=32 << 20),
        cost_estimate=pl.CostEstimate(
            flops=4 * cut * width * routed, bytes_accessed=20 * cut * width, transcendentals=cut * routed
        ),
    )(got, act2, middle, dy_slice, chosen, router, gain)


def out_kernel(where_ref, hid_ref, down_ref, near_ref, far_ref):
    p = pl.program_id(0)
    value = nn(hid_ref[...], down_ref[...]).astype(bf16)

    @pl.when(p % 2 == 0)
    def _():
        near_ref[0] = value

    @pl.when(p % 2 == 1)
    def _():
        far_ref[0] = value


def out_pieces(hid, down, blocks, homes, piece_rows):
    hidden, width = down.shape
    count = lax.axis_size(T)
    n_slab = piece_rows // SLAB
    where = jnp.concatenate([jnp.asarray(blocks, jnp.int32), homes])
    n = len(blocks)
    home = lambda p, w: (w[n + p // 2], (p // 2) % n_slab, 0)
    return pl.pallas_call(
        out_kernel,
        grid_spec=pltpu.PrefetchScalarGridSpec(
            num_scalar_prefetch=1,
            grid=(n,),
            in_specs=[
                pl.BlockSpec((SLAB, hidden), lambda p, w: (w[p], 0)),
                pl.BlockSpec((hidden, width), lambda p, w: (0, 0), pipeline_mode=pl.Buffered(1)),
            ],
            out_specs=[pl.BlockSpec((1, SLAB, width), home)] * 2,
        ),
        out_shape=[jax.ShapeDtypeStruct((count, piece_rows, width), bf16)] * 2,
        compiler_params=pltpu.CompilerParams(vmem_limit_bytes=32 << 20),
        cost_estimate=pl.CostEstimate(flops=1000, bytes_accessed=1000, transcendentals=0),
    )(where, hid, down)


def sum_t_permute(v):
    count = lax.axis_size(T)
    cut = v.shape[0] // count
    t = lax.axis_index(T)
    low = v.astype(bf16)
    block = lambda k: lax.dynamic_slice(low, ((t ^ k) * cut, 0), (cut, v.shape[1]))
    total = block(0).astype(f32)
    for k in range(1, count):
        total = total + across(block(k), k).astype(f32)
    return total


def body(
    hidden_in,
    segment_ids,
    expert_ids,
    capacity,
    norm_attn,
    norm_ffn,
    norm_query,
    norm_key,
    w_query,
    w_key,
    w_value,
    w_out,
    w_router,
    w_gate,
    w_up,
    w_down,
    grad_out,
):
    micro, _, span, width = hidden_in.shape
    rows = micro * span
    hd = norm_query.shape[0]
    topk = expert_ids.shape[3]
    experts = w_router.shape[1]
    mine = w_gate.shape[0]
    nb, nc, nt_ = lax.axis_size(B), lax.axis_size(C), lax.axis_size(T)
    sources = nb * nc
    cut = rows // nt_
    b, c, t = lax.axis_index(B), lax.axis_index(C), lax.axis_index(T)
    place = b * nc + c
    seq = span * nc
    back = (seq // 2 - 1 + span - 1) // span
    heads = w_query.shape[1] // hd
    q_cols = heads * hd
    scale = hd ** (-0.5)
    routed = -(-experts // 128) * 128

    x = hidden_in.reshape(rows, width)
    dy = grad_out.reshape(rows, width)

    w_qkv = lax.all_gather(
        jnp.concatenate([w_query, w_key, w_value], axis=1), BC, axis=0, tiled=True
    )
    ids_own = expert_ids.reshape(rows, topk).T
    info = jnp.concatenate([ids_own, segment_ids.reshape(1, rows)], axis=0)
    info = jnp.pad(info, ((0, -(-(topk + 1) // 8) * 8 - topk - 1), (0, 0)))
    tall = info.shape[0]
    info = lax.all_to_all(jnp.concatenate([info] * sources, axis=0), BC, 0, 0, tiled=True)
    info = info.reshape(sources, tall, rows)
    ids_all = info[:, :topk]
    seg_all = info[:, topk].reshape(nb, nc, micro, span)
    local = place * mine + jnp.arange(mine)
    hot = jnp.sum((ids_all[:, :, None, :] == local[None, None, :, None]).astype(f32), axis=1)
    hot = hot.reshape(sources, mine, micro, span)
    upper = (jnp.arange(span)[:, None] < jnp.arange(span)[None, :]).astype(bf16)
    within = nn(hot.astype(bf16).reshape(-1, span), upper).reshape(hot.shape)
    totals = jnp.sum(hot, axis=-1)
    earlier = jnp.arange(sources)[:, None] < jnp.arange(sources)[None, :]
    before = jnp.sum(jnp.where(earlier[:, :, None, None], totals[:, None], 0.0), axis=0)
    rank = within + before[..., None]
    room = lax.dynamic_slice(capacity, (place * mine,), (mine,)).astype(f32)
    kept = jnp.where(rank < room[None, :, None, None], hot, 0.0)
    kept = kept.reshape(nb, nc, mine, nt_, cut).transpose(0, 3, 1, 4, 2).reshape(-1, mine)
    ids_rows = ids_all.reshape(nb, nc, topk, nt_, cut).transpose(0, 3, 1, 4, 2).reshape(-1, topk)
    names = jnp.arange(routed)
    marks = jnp.sum((ids_rows[:, :, None] == names).astype(f32), axis=1)
    for e in range(mine):
        marks = marks + jnp.where(names[None, :] == place * mine + e, kept[:, e : e + 1], 0.0)
    piece_rows = nc * cut
    marks = marks.reshape(nb * nt_, piece_rows, routed)
    total_rows = nb * nt_ * piece_rows
    ids_slice = lax.dynamic_slice(expert_ids.reshape(rows, topk), (t * cut, 0), (cut, topk))
    chosen = jnp.sum((ids_slice[:, :, None] == names).astype(f32), axis=1)

    xf = x.astype(f32)
    act1 = (xf * inv_rms(xf) * norm_attn).astype(bf16)
    positions = c * span + jnp.arange(span)
    cosine, sine = angles(positions, hd)
    cosine = jnp.concatenate([cosine] * micro, axis=0)
    sine = jnp.concatenate([sine] * micro, axis=0)
    act1_slice = lax.dynamic_slice(act1, (t * cut, 0), (cut, width))
    own_cols = width // sources

    def columns(v):
        v = gather_t(to_features(v)).reshape(nt_, sources, cut, own_cols)
        return v.transpose(1, 0, 2, 3).reshape(-1, own_cols)

    act1_cols = columns(act1_slice)
    w_or = jnp.concatenate([w_out, pad_cols(w_router, routed)], axis=1)
    w_qkv, w_or, marks, act1, act1_cols, cosine, sine = after(
        w_qkv, w_or, marks, act1, act1_cols, cosine, sine
    )
    w_or = lax.all_gather(w_or, BC, axis=0, tiled=True)
    dy_slice = lax.dynamic_slice(dy, (t * cut, 0), (cut, width))
    dy_tied, w_or = after(dy_slice, w_or)
    dy_own = gather_c(dy_tied)
    out_w = w_or[:, :q_cols]
    router_wide = w_or[:, q_cols:]
    router_w = router_wide[:, :experts]
    n_slab = piece_rows // SLAB
    groups = ((0,), 6 * piece_rows), ((1, 2, 3), 0)
    hidden = mine * w_gate.shape[1]
    gate_w = w_gate.reshape(hidden, width)
    up_w = w_up.reshape(hidden, width)
    down_w = w_down.reshape(hidden, width)
    qkv = nn(act1, w_qkv)
    q_raw = qkv[:, :q_cols].reshape(rows, heads, hd)
    k_raw = qkv[:, q_cols : q_cols + hd]
    q = heads_forward(q_raw, norm_query, cosine[:, None], sine[:, None])
    k = heads_forward(k_raw, norm_key, cosine, sine)
    kv = jnp.concatenate([k, qkv[:, q_cols + hd :].astype(bf16)], axis=1)
    blocks = [
        lax.ppermute(kv, C, [(i, i + s) for i in range(nc - s)]) for s in range(back, 0, -1)
    ]
    window = jnp.stack(blocks + [kv]).reshape(back + 1, micro, span, 2 * hd)
    window = window.transpose(1, 0, 2, 3).reshape(micro, (back + 1) * span, 2 * hd)
    keys, values = window[..., :hd], window[..., hd:]
    seg_seq = lax.dynamic_index_in_dim(seg_all, b, 0, False)
    seg_seq = jnp.pad(seg_seq, ((back, 0), (0, 0), (0, 0)), constant_values=-1)
    seg_win = lax.dynamic_slice(seg_seq, (c, 0, 0), (back + 1, micro, span))
    seg_win = seg_win.transpose(1, 0, 2).reshape(micro, -1)
    seg_own = segment_ids.reshape(micro, span)
    allowed = (seg_own[:, :, None] == seg_win[:, None, :]) & (
        jnp.arange((back + 1) * span)[None, None, :] <= back * span + jnp.arange(span)[None, :, None]
    )
    qg = q.reshape(micro, span, heads, hd).transpose(0, 2, 1, 3)
    qg = qg.reshape(micro, heads * span, hd)
    scores = bdot(qg, keys, 2, 2).reshape(micro, heads, span, -1) * scale
    bias = jnp.where(allowed, 0.0, -1e30)
    side = jnp.where(jnp.arange(hd) < hd // 2, -1.0, 1.0)
    cos_own, sin_own = cosine[:span], sine[:span] * side
    scores = scores + bias[:, None]
    top = jnp.max(scores, axis=-1, keepdims=True)
    weight = jnp.exp(scores - top)
    total = jnp.sum(weight, axis=-1, keepdims=True)
    probs = weight / total
    probs_low = probs.astype(bf16).reshape(micro, heads * span, -1)
    mixed = bdot(probs_low, values, 2, 1).astype(bf16).reshape(micro, heads, span, hd)
    mixed = mixed.transpose(0, 2, 1, 3).reshape(rows, q_cols)
    branch = sum_t_permute(nt(mixed, out_w))
    x_slice = lax.dynamic_slice(x, (t * cut, 0), (cut, width)).astype(f32)
    middle = x_slice + branch
    r2 = inv_rms(middle)
    act2 = (middle * r2 * norm_ffn).astype(bf16)
    dy_own, act2 = after(dy_own, act2)
    act2_own = gather_c(act2)
    dy_plane = lax.all_gather(dy_own, T, axis=0, tiled=True)
    mixed_later, act2_own, router_wide = after(mixed, act2_own, router_wide)
    mixed_all = lax.all_gather(mixed_later, BC, axis=0, tiled=True)

    places = (
        jnp.arange(routed)[:, None] == place * mine + jnp.arange(hidden)[None, :] // w_gate.shape[1]
    ).astype(bf16)
    consts = (router_wide, places, gate_w, up_w, down_w)

    def experts_on(group, base, near, dys, held):
        pairs = [(side, k) for side in (0, 1) for k in group]
        where = [(b ^ side) * nt_ + (t ^ k) for side, k in pairs]
        where += [(t ^ k) * (dys[0].shape[0] // (nt_ * piece_rows)) for side, k in pairs]
        acts = near + [swap(v) for v in near]
        return expert_pieces(base, jnp.stack(where), acts, dys, marks, consts, held, total_rows)

    half = piece_rows // 2
    from_x, from_y = across(act2_own, 1), across(act2_own, 2)
    held, own_sums = experts_on((0,), 6 * piece_rows, [act2_own], [dy_own, swap(dy_own)], None)
    *held, from_x, from_y, dy_plane = after(*held, from_x, from_y, dy_plane)
    low, high = across(from_x[:half], 2), across(from_y[half:], 1)
    corner = jnp.concatenate([low, high], axis=0)
    held, sums = experts_on((1, 2, 3), 0, [from_x, from_y, corner], [dy_plane, swap(dy_plane)], held)
    ring_sums, corner_sums = [v[:2] for v in sums], [v[2:] for v in sums]
    act_all, dy_all, hid_gated, d_gate, d_up = held
    d_in_plane, (hid_later, act2_later) = sum_plane(
        own_sums, ring_sums, corner_sums, (hid_gated, act2)
    )
    blocks, homes = [], []
    for g, start in groups:
        for n, k in enumerate(g):
            for i in range(n_slab):
                first = start // SLAB + i * 2 * len(g) + n
                blocks += [first, first + len(g)]
                homes.append(t ^ k)
    out_near, out_far = out_pieces(hid_later, down_w, blocks, jnp.stack(homes), piece_rows)
    d_in_plane, out_near, out_far, mixed_all = after(d_in_plane, out_near, out_far, mixed_all)
    d_in_got = send_c(d_in_plane)
    out_chip = add_low(out_near, swap(out_far)).reshape(-1, width)
    grad_up = tn(d_up, act_all)
    d_in_got, grad_up, out_chip = after(d_in_got, grad_up, out_chip)
    out_plane = lax.psum_scatter(out_chip, T, scatter_dimension=0, tiled=True)

    d_norm, d_branch_slice, d_logits, gain_ffn = turn_back(
        experts, d_in_got, act2_later, middle, dy_slice, chosen, router_wide, norm_ffn[None]
    )
    d_branch = gather_t(d_branch_slice)
    grad_gate = tn(d_gate, act_all)
    d_branch, grad_gate, act2_late, d_logits = after(d_branch, grad_gate, act2_later, d_logits)
    d_branch_cols = to_features(d_branch)
    devices = sources * nt_
    router_part = tn(act2_late, d_logits)[:, :experts]

    d_mixed = nn(d_branch, out_w).astype(bf16)
    d_q, d_window, gain_q = attend_back(
        q.reshape(rows, q_cols), qkv, window, bias, d_mixed, cos_own, sin_own, norm_query[None]
    )
    d_window, out_plane = after(d_window, out_plane)
    out_sum = sum_c_permute(out_plane)
    d_kv = d_window.reshape(micro, back + 1, span, 2 * hd)
    d_kv_own = d_kv[:, back].reshape(rows, 2 * hd).astype(f32)
    for s in range(1, back + 1):
        piece = d_kv[:, back - s].reshape(rows, 2 * hd)
        d_kv_own = d_kv_own + lax.ppermute(piece, C, [(i + s, i) for i in range(nc - s)]).astype(f32)
    d_k_raw, gain_k_rows = heads_back(k_raw, norm_key, cosine, sine, d_kv_own[:, :hd])
    gain_k = jnp.sum(gain_k_rows, axis=0)
    d_qkv = jnp.concatenate([d_q, d_k_raw.astype(bf16), d_kv_own[:, hd:].astype(bf16)], axis=1)
    d_qkv, out_sum, d_branch_cols = after(d_qkv, out_sum, d_branch_cols)
    late = lax.all_gather(d_qkv, BC, axis=0, tiled=True)
    d_act1 = sum_t(nt(d_qkv, w_qkv))
    d_norm1, gain1_rows = norm_back(x_slice, inv_rms(x_slice), norm_attn, d_act1)
    gain_attn = jnp.sum(gain1_rows, axis=0)

    pieces = [v.reshape(devices, -1) for v in (router_part, gain_attn, gain_ffn, gain_q, gain_k)]
    sizes = [v.shape[1] for v in pieces]
    flat = jnp.concatenate(pieces, axis=1).astype(bf16)
    flat = lax.all_to_all(pad_cols(flat, -(-flat.shape[1] // 128) * 128), ALL, 0, 0, tiled=True)
    flat = jnp.sum(flat.astype(f32), axis=0, keepdims=True)
    lines = -(-flat.shape[1] // width)
    flat = pad_cols(flat, lines * width).reshape(lines, width)
    flat = jnp.pad(flat, ((0, -lines % 16), (0, 0)))
    final = jnp.concatenate([branch + out_sum, d_norm + d_norm1, flat], axis=0).astype(bf16)
    final, dy_all, mixed_all = after(final, dy_all, mixed_all)
    final = gather_t(final).astype(f32).reshape(nt_, -1, width)
    hidden_out = final[:, :cut].reshape(rows, width) + xf
    grad_in = final[:, cut : 2 * cut].reshape(rows, width) + dy.astype(f32)
    flat = final[:, 2 * cut : 2 * cut + lines].reshape(nt_, lines * width)
    gains, start = [], 0
    for size in sizes:
        gains.append(flat[:, start : start + size].reshape(-1))
        start += size
    grad_router = gains.pop(0).reshape(-1, experts)
    grad_down = tn(hid_gated, dy_all)
    grad_out_w = tn(d_branch_cols, mixed_all)
    grad_qkv = tn(act1_cols, late)
    shape = hidden_in.shape
    return (
        hidden_out.reshape(shape),
        grad_in.reshape(shape),
        gains[0],
        gains[1],
        gains[2],
        gains[3],
        grad_qkv[:, :q_cols],
        grad_qkv[:, q_cols : q_cols + hd],
        grad_qkv[:, q_cols + hd :],
        grad_out_w,
        grad_router,
        grad_gate.reshape(w_gate.shape),
        grad_up.reshape(w_up.shape),
        grad_down.reshape(w_down.shape),
    )


def solution(mesh):
    rows = P(None, B, C, None)
    ids = P(None, B, C)
    whole = P()
    matrix = P(BC, T)
    router = P(BC, None)
    expert = P(BC, T, None)
    vector = P(BC)
    in_specs = (rows, ids, rows) + (whole,) * 5 + (matrix,) * 4 + (router,) + (expert,) * 3 + (rows,)
    out_specs = (rows, rows) + (vector,) * 4 + (matrix,) * 4 + (router,) + (expert,) * 3
    return jax.shard_map(body, mesh=mesh, in_specs=in_specs, out_specs=out_specs, check_vma=False)
```

```python
import functools

import jax
import jax.numpy as jnp
from jax import lax
from jax.experimental import pallas as pl
from jax.experimental.pallas import tpu as pltpu
from jax.sharding import PartitionSpec as P

B, C, T = "batch", "ctx", "tensor"
BC = (B, C)
ALL = (B, C, T)
f32 = jnp.float32
bf16 = jnp.bfloat16
EPS = 1e-06


def dot(a, b, ca, cb):
    return lax.dot_general(a, b, (((ca,), (cb,)), ((), ())), preferred_element_type=f32)


def nn(a, b):
    return dot(a, b, 1, 0)


def nt(a, b):
    return dot(a, b, 1, 1)


def tn(a, b):
    return dot(a, b, 0, 0)


def bdot(a, b, ca, cb):
    return lax.dot_general(a, b, (((ca,), (cb,)), ((0,), (0,))), preferred_element_type=f32)


def after(*values):
    return lax.optimization_barrier(values)


def pad_cols(v, width):
    return jnp.pad(v, ((0, 0), (0, width - v.shape[1])))


def inv_rms(v):
    return lax.rsqrt(jnp.mean(v * v, axis=-1, keepdims=True) + EPS)


def turn(v):
    half = v.shape[-1] // 2
    return jnp.concatenate([-v[..., half:], v[..., :half]], axis=-1)


def angles(positions, width):
    half = width // 2
    frequency = jnp.power(1000000.0, -(2.0 * jnp.arange(half, dtype=f32)) / width)
    phases = positions.astype(f32)[:, None] * frequency[None, :]
    phases = jnp.concatenate([phases, phases], axis=-1)
    return jnp.cos(phases), jnp.sin(phases)


def norm_back(v, r, gain, grad):
    scaled = gain * grad
    grad_v = r * scaled - v * (r * r * r) * jnp.mean(v * scaled, axis=-1, keepdims=True)
    return grad_v, grad * v * r


def heads_forward(raw, gain, cosine, sine):
    v = raw * inv_rms(raw) * gain
    return (v * cosine + turn(v) * sine).astype(bf16)


def heads_back(raw, gain, cosine, sine, grad):
    grad = grad * cosine - turn(grad) * sine
    return norm_back(raw, inv_rms(raw), gain, grad)


def gather_t(v):
    count = lax.axis_size(T)
    return lax.all_to_all(jnp.concatenate([v] * count, axis=0), T, 0, 0, tiled=True)


def sum_t(v):
    count = lax.axis_size(T)
    got = lax.all_to_all(v.astype(bf16), T, 0, 0, tiled=True)
    got = got.reshape(count, v.shape[0] // count, v.shape[1])
    return jnp.sum(got.astype(f32), axis=0)


def swap(v):
    return lax.ppermute(v, B, [(0, 1), (1, 0)])


def across(v, k):
    return lax.ppermute(v, T, [(i, i ^ k) for i in range(lax.axis_size(T))])


def add_low(*parts):
    total = parts[0].astype(f32)
    for part in parts[1:]:
        total = total + part.astype(f32)
    return total.astype(bf16)


def gather_c(v):
    count = lax.axis_size(C)
    return lax.all_to_all(jnp.concatenate([v] * count, axis=0), C, 0, 0, tiled=True)


def spread_plane(own):
    half = own.shape[0] // 2
    from_x, from_y = across(own, 1), across(own, 2)
    low, high = across(from_x[:half], 2), across(from_y[half:], 1)
    return [own, from_x, from_y, jnp.concatenate([low, high], axis=0)]


def sum_plane(own, ring, corner, held=()):
    diagonal = add_low(corner[0][0], swap(corner[1])[0])
    half = diagonal.shape[0] // 2
    from_x, from_y = across(diagonal[:half], 1), across(diagonal[half:], 2)
    ring_far = swap(ring[1])
    own_far = swap(own[1])
    from_x, from_y, *held = after(from_x, from_y, *held)
    east = add_low(ring[0][0], ring_far[0])
    north = add_low(ring[0][1], ring_far[1])
    east = jnp.concatenate([east[:half], add_low(east[half:], from_y)], axis=0)
    north = jnp.concatenate([add_low(north[:half], from_x), north[half:]], axis=0)
    return add_low(own[0][0], own_far[0], across(east, 1), across(north, 2)), held


def to_features(v):
    return lax.all_to_all(v, BC, 1, 0, tiled=True)


def send_c(plane):
    count = lax.axis_size(C)
    got = lax.all_to_all(plane, C, 0, 0, tiled=True)
    return got.reshape(count, plane.shape[0] // count, plane.shape[1])


SLAB = 256


def sum_c_permute(plane):
    count = lax.axis_size(C)
    cut = plane.shape[0] // count
    c = lax.axis_index(C)
    block = lambda k: lax.dynamic_slice(plane, (((c + k) % count) * cut, 0), (cut, plane.shape[1]))
    total = block(0).astype(f32)
    for k in range(1, count):
        got = lax.ppermute(block(k), C, [(i, (i + k) % count) for i in range(count)])
        total = total + got.astype(f32)
    return total


def expert_kernel(count, first, where_ref, *refs):
    acts, dys, marks = refs[:count], refs[count : count + 2], refs[count + 2 : 2 * count + 2]
    router_ref, place_ref = refs[2 * count + 2 : 2 * count + 4]
    weights_hbm = refs[2 * count + 4 : 2 * count + 7]
    act_b, dy_b, hid_b, dg_b, du_b, din_b, mark_b = refs[-13:-6]
    gate_w, up_w, down_w = refs[-6:-3]
    in_sem, w_sem, out_sem = refs[-3:]
    sizes = [min(2, count // 2)] + [1] * (count // 2 > 2)
    outs = refs[-18 - 2 * len(sizes) : -13]
    act_all, dy_all, hid_all, dg_all, du_all = outs[:5]
    given, low_p = [], 0
    for size, to in zip(sizes * 2, outs[5:]):
        given.append((low_p, size, to))
        low_p += size
    i = pl.program_id(0)
    width = act_b.shape[2]
    hidden = gate_w.shape[0]
    src = pl.ds(pl.multiple_of(i * SLAB, SLAB), SLAB)
    base = first + i * count * SLAB
    stored = ((act_b, act_all), (dy_b, dy_all), (hid_b, hid_all), (dg_b, dg_all), (du_b, du_all))
    weights = [
        pltpu.make_async_copy(v, w, w_sem.at[k])
        for k, (v, w) in enumerate(zip(weights_hbm, (gate_w, up_w, down_w)))
    ]

    piece = pl.num_programs(0) * SLAB

    def load(k, p):
        if k == 0:
            return pltpu.make_async_copy(acts[p].at[src], act_b.at[p], in_sem.at[0, p])
        rows = pl.ds(pl.multiple_of(where_ref[count + p] * piece + i * SLAB, SLAB), SLAB)
        return pltpu.make_async_copy(dys[p // (count // 2)].at[rows], dy_b.at[p], in_sem.at[1, p])

    def stores(p):
        rows = pl.ds(pl.multiple_of(base + p * SLAB, SLAB), SLAB)
        return [
            pltpu.make_async_copy(v.at[p], to.at[rows], out_sem.at[k, p])
            for k, (v, to) in enumerate(stored)
        ]

    def give(p, place, to):
        return pltpu.make_async_copy(din_b.at[p], to.at[place, src], out_sem.at[5, p])

    load(0, 0).start()

    @pl.when(i == 0)
    def _():
        weights[0].start()
        weights[1].start()

    load(1, 0).start()

    @pl.when(i == 0)
    def _():
        weights[2].start()

    for p in range(1, count):
        load(0, p).start()
        load(1, p).start()
    for p in range(count):
        mark_b[p] = marks[p][0]

    @pl.when(i == 0)
    def _():
        weights[0].wait()
        weights[1].wait()

    def one(p, carry):
        for k, buffer in enumerate((act_b, dy_b)):
            pltpu.make_async_copy(acts[0].at[src], buffer.at[p], in_sem.at[k, p]).wait()
        act = act_b[p]
        mark = mark_b[p]
        logits = nn(act, router_ref[...])
        top = jnp.max(jnp.where(mark > 0.5, logits, -1e30), axis=1, keepdims=True)
        parts = jnp.where(mark > 0.5, jnp.exp(logits - top), 0.0)
        parts = parts / jnp.sum(parts, axis=1, keepdims=True)
        gates = jnp.where(mark > 1.5, parts, 0.0)
        high = gates.astype(bf16)
        low = (gates - high.astype(f32)).astype(bf16)

        @pl.when((p == 0) & (i == 0))
        def _():
            weights[2].wait()

        place = place_ref[...]
        wide = nn(high, place) + nn(low, place)
        gate = nt(act, gate_w[...])
        up = nt(act, up_w[...])
        dyw = nt(dy_b[p], down_w[...])
        sig = 0.5 * jnp.tanh(0.5 * gate) + 0.5
        silu = gate * sig
        hid = silu * up
        hid_b[p] = (wide * hid).astype(bf16)
        share = nt((hid * dyw).astype(bf16), place)
        d_hid = wide * dyw
        dg_b[p] = (d_hid * up * (sig + silu * (1.0 - sig))).astype(bf16)
        du_b[p] = (d_hid * silu).astype(bf16)
        din_b[p, :, width:] = jnp.where(mark > 1.5, share, 0.0).astype(bf16)
        for w in range(0, width, 512):
            cols = slice(w, w + 512)
            total = nn(dg_b[p], gate_w[:, cols]) + nn(du_b[p], up_w[:, cols])
            din_b[p, :, cols] = total.astype(bf16)
        for copy in stores(p):
            copy.start()

        for low_p, size, to in given:

            @pl.when((p >= low_p) & (p < low_p + size))
            def _(low_p=low_p, to=to):
                give(p, p - low_p, to).start()

        return carry

    lax.fori_loop(0, count, one, 0)
    for p in range(count):
        for copy in stores(p):
            copy.wait()
        for low_p, size, to in given:
            if low_p <= p < low_p + size:
                give(p, p - low_p, to).wait()


def expert_pieces(first, where, acts, dys, marks, consts, held, total_rows):
    count = len(acts)
    rows, width = acts[0].shape
    hidden = consts[2].shape[0]
    routed = consts[0].shape[1]
    left = pl.BlockSpec(memory_space=pl.ANY)
    in_specs = [left] * (count + 2)
    in_specs += [
        pl.BlockSpec((1, SLAB, routed), lambda i, w, p=p: (w[p], i, 0)) for p in range(count)
    ]
    in_specs += [
        pl.BlockSpec(v.shape, lambda i, w: (0, 0), pipeline_mode=pl.Buffered(1)) for v in consts[:2]
    ]
    in_specs += [left] * 3
    out_shape = [jax.ShapeDtypeStruct((total_rows, width), bf16)] * 2
    out_shape += [jax.ShapeDtypeStruct((total_rows, hidden), bf16)] * 3
    sizes = [min(2, count // 2)] + [1] * (count // 2 > 2)
    out_shape += [jax.ShapeDtypeStruct((size, rows, width + routed), bf16) for size in sizes * 2]
    args = [where, *acts, *dys, *([marks] * count), *consts]
    aliases = {}
    if held is not None:
        for k, v in enumerate(held):
            aliases[len(args)] = k
            args.append(v)
            in_specs.append(left)
    outs = pl.pallas_call(
        functools.partial(expert_kernel, count, first),
        grid_spec=pltpu.PrefetchScalarGridSpec(
            num_scalar_prefetch=1,
            grid=(rows // SLAB,),
            in_specs=in_specs,
            out_specs=[left] * len(out_shape),
            scratch_shapes=[pltpu.VMEM((count, SLAB, width), bf16)] * 2
            + [pltpu.VMEM((count, SLAB, hidden), bf16)] * 3
            + [pltpu.VMEM((count, SLAB, width + routed), bf16)]
            + [pltpu.VMEM((count, SLAB, routed), f32)]
            + [pltpu.VMEM((hidden, width), bf16)] * 3
            + [pltpu.SemaphoreType.DMA((2, count))]
            + [pltpu.SemaphoreType.DMA((3,))]
            + [pltpu.SemaphoreType.DMA((6, count))],
        ),
        out_shape=out_shape,
        input_output_aliases=aliases,
        compiler_params=pltpu.CompilerParams(vmem_limit_bytes=56 << 20),
        cost_estimate=pl.CostEstimate(flops=1000, bytes_accessed=1000, transcendentals=0),
    )(*args)
    return outs[:5], outs[5:]


def attend_back_kernel(heads, scale, q_ref, raw_ref, kv_ref, bias_ref, dm_ref, cos_ref, sin_ref, gain_ref, dq_ref, dkv_ref, gq_ref, rows_q, rows_m, rows_p, rows_s):
    span = q_ref.shape[0]
    hd = gain_ref.shape[1]
    keys, values = kv_ref[0, :, :hd], kv_ref[0, :, hd:]
    bias = bias_ref[0]
    cosine, sine = cos_ref[...], sin_ref[...]
    gain = gain_ref[...]

    @pl.when(pl.program_id(0) == 0)
    def _():
        gq_ref[...] = jnp.zeros_like(gq_ref)

    total = jnp.zeros((1, hd), f32)
    for h in range(heads):
        cols = slice(h * hd, (h + 1) * hd)
        lines = slice(h * span, (h + 1) * span)
        q = q_ref[:, cols]
        dm = dm_ref[:, cols]
        rows_q[lines, :] = q
        rows_m[lines, :] = dm
        scores = nt(q, keys) * scale + bias
        weight = jnp.exp(scores - jnp.max(scores, axis=1, keepdims=True))
        probs = weight / jnp.sum(weight, axis=1, keepdims=True)
        d_probs = nt(dm, values)
        d_scores = probs * (d_probs - jnp.sum(probs * d_probs, axis=1, keepdims=True))
        low = d_scores.astype(bf16)
        rows_p[lines, :] = probs.astype(bf16)
        rows_s[lines, :] = low
        d_q = nn(low, keys) * scale
        grad = d_q * cosine - pltpu.roll(d_q, hd // 2, 1) * sine
        raw = raw_ref[:, cols]
        d_raw, gain_rows = norm_back(raw, inv_rms(raw), gain, grad)
        dq_ref[:, cols] = d_raw.astype(bf16)
        total = total + jnp.sum(gain_rows, axis=0, keepdims=True)
    gq_ref[...] += total
    dkv_ref[0, :, :hd] = (tn(rows_s[...], rows_q[...]) * scale).astype(bf16)
    dkv_ref[0, :, hd:] = tn(rows_p[...], rows_m[...]).astype(bf16)


def attend_back(q, qkv, window, bias, d_mixed, cosine, sine, gain):
    micro, reach, pair = window.shape
    hd = pair // 2
    span, q_cols = q.shape[0] // micro, q.shape[1]
    heads = q_cols // hd
    row = lambda m: (m, 0)
    flat = lambda m: (0, 0)
    deep = lambda m: (m, 0, 0)
    return pl.pallas_call(
        functools.partial(attend_back_kernel, heads, hd ** (-0.5)),
        grid=(micro,),
        in_specs=[
            pl.BlockSpec((span, q_cols), row),
            pl.BlockSpec((span, q_cols), row),
            pl.BlockSpec((1, reach, pair), deep),
            pl.BlockSpec((1, span, reach), deep),
            pl.BlockSpec((span, q_cols), row),
            pl.BlockSpec((span, hd), flat),
            pl.BlockSpec((span, hd), flat),
            pl.BlockSpec((1, hd), flat),
        ],
        out_specs=[
            pl.BlockSpec((span, q_cols), row),
            pl.BlockSpec((1, reach, pair), deep),
            pl.BlockSpec((1, hd), flat),
        ],
        out_shape=[
            jax.ShapeDtypeStruct(q.shape, bf16),
            jax.ShapeDtypeStruct(window.shape, bf16),
            jax.ShapeDtypeStruct((1, hd), f32),
        ],
        scratch_shapes=[pltpu.VMEM((heads * span, hd), bf16)] * 2
        + [pltpu.VMEM((heads * span, reach), bf16)] * 2,
        compiler_params=pltpu.CompilerParams(vmem_limit_bytes=32 << 20),
        cost_estimate=pl.CostEstimate(
            flops=10 * micro * heads * span * reach * hd,
            bytes_accessed=10 * micro * span * q_cols,
            transcendentals=micro * heads * span * reach,
        ),
    )(q, qkv, window, bias, d_mixed, cosine, sine, gain)


def turn_back_kernel(experts, got_ref, act_ref, mid_ref, dy_ref, chosen_ref, router_ref, gain_ref, dn_ref, low_ref, dl_ref, gain_out):
    width = mid_ref.shape[1]
    total = got_ref[0].astype(f32)
    for k in range(1, got_ref.shape[0]):
        total = total + got_ref[k].astype(f32)
    d_gates = total[:, width:]
    router = router_ref[...]
    chosen = chosen_ref[...]
    logits = nn(act_ref[...], router)
    real = lax.broadcasted_iota(jnp.int32, logits.shape, 1) < experts
    logits = jnp.where(real, logits, -1e30)
    weight = jnp.exp(logits - jnp.max(logits, axis=1, keepdims=True))
    probs = weight / jnp.sum(weight, axis=1, keepdims=True)
    picked = probs * chosen
    picked_sum = jnp.sum(picked, axis=1, keepdims=True)
    lean = jnp.sum(d_gates * picked / picked_sum, axis=1, keepdims=True)
    c_grad = chosen * (d_gates - lean) / picked_sum
    d_logits = probs * (c_grad - jnp.sum(probs * c_grad, axis=1, keepdims=True))
    d_logits = jnp.where(real, d_logits, 0.0).astype(bf16)
    dl_ref[...] = d_logits
    d_act = total[:, :width] + nt(d_logits, router)
    middle = mid_ref[...]
    d_norm, gain_rows = norm_back(middle, inv_rms(middle), gain_ref[...], d_act)
    dn_ref[...] = d_norm
    low_ref[...] = (dy_ref[...].astype(f32) + d_norm).astype(bf16)
    gain_out[...] = jnp.sum(gain_rows, axis=0, keepdims=True)


def turn_back(experts, got, act2, middle, dy_slice, chosen, router, gain):
    cut, width = middle.shape
    routed = router.shape[1]
    return pl.pallas_call(
        functools.partial(turn_back_kernel, experts),
        out_shape=[
            jax.ShapeDtypeStruct((cut, width), f32),
            jax.ShapeDtypeStruct((cut, width), bf16),
            jax.ShapeDtypeStruct((cut, routed), bf16),
            jax.ShapeDtypeStruct((1, width), f32),
        ],
        compiler_params=pltpu.CompilerParams(vmem_limit_bytes=32 << 20),
        cost_estimate=pl.CostEstimate(
            flops=4 * cut * width * routed, bytes_accessed=20 * cut * width, transcendentals=cut * routed
        ),
    )(got, act2, middle, dy_slice, chosen, router, gain)


def out_kernel(where_ref, hid_ref, down_ref, near_ref, far_ref):
    p = pl.program_id(0)
    value = nn(hid_ref[...], down_ref[...]).astype(bf16)

    @pl.when(p % 2 == 0)
    def _():
        near_ref[0] = value

    @pl.when(p % 2 == 1)
    def _():
        far_ref[0] = value


def out_pieces(hid, down, blocks, homes, piece_rows):
    hidden, width = down.shape
    count = lax.axis_size(T)
    n_slab = piece_rows // SLAB
    where = jnp.concatenate([jnp.asarray(blocks, jnp.int32), homes])
    n = len(blocks)
    home = lambda p, w: (w[n + p // 2], (p // 2) % n_slab, 0)
    return pl.pallas_call(
        out_kernel,
        grid_spec=pltpu.PrefetchScalarGridSpec(
            num_scalar_prefetch=1,
            grid=(n,),
            in_specs=[
                pl.BlockSpec((SLAB, hidden), lambda p, w: (w[p], 0)),
                pl.BlockSpec((hidden, width), lambda p, w: (0, 0), pipeline_mode=pl.Buffered(1)),
            ],
            out_specs=[pl.BlockSpec((1, SLAB, width), home)] * 2,
        ),
        out_shape=[jax.ShapeDtypeStruct((count, piece_rows, width), bf16)] * 2,
        compiler_params=pltpu.CompilerParams(vmem_limit_bytes=32 << 20),
        cost_estimate=pl.CostEstimate(flops=1000, bytes_accessed=1000, transcendentals=0),
    )(where, hid, down)


def sum_t_permute(v):
    count = lax.axis_size(T)
    cut = v.shape[0] // count
    t = lax.axis_index(T)
    low = v.astype(bf16)
    block = lambda k: lax.dynamic_slice(low, ((t ^ k) * cut, 0), (cut, v.shape[1]))
    total = block(0).astype(f32)
    for k in range(1, count):
        total = total + across(block(k), k).astype(f32)
    return total


def body(
    hidden_in,
    segment_ids,
    expert_ids,
    capacity,
    norm_attn,
    norm_ffn,
    norm_query,
    norm_key,
    w_query,
    w_key,
    w_value,
    w_out,
    w_router,
    w_gate,
    w_up,
    w_down,
    grad_out,
):
    micro, _, span, width = hidden_in.shape
    rows = micro * span
    hd = norm_query.shape[0]
    topk = expert_ids.shape[3]
    experts = w_router.shape[1]
    mine = w_gate.shape[0]
    nb, nc, nt_ = lax.axis_size(B), lax.axis_size(C), lax.axis_size(T)
    sources = nb * nc
    cut = rows // nt_
    b, c, t = lax.axis_index(B), lax.axis_index(C), lax.axis_index(T)
    place = b * nc + c
    seq = span * nc
    back = (seq // 2 - 1 + span - 1) // span
    heads = w_query.shape[1] // hd
    q_cols = heads * hd
    scale = hd ** (-0.5)
    routed = -(-experts // 128) * 128

    x = hidden_in.reshape(rows, width)
    dy = grad_out.reshape(rows, width)

    w_qkv = lax.all_gather(
        jnp.concatenate([w_query, w_key, w_value], axis=1), BC, axis=0, tiled=True
    )
    ids_own = expert_ids.reshape(rows, topk).T
    info = jnp.concatenate([ids_own, segment_ids.reshape(1, rows)], axis=0)
    info = jnp.pad(info, ((0, -(-(topk + 1) // 8) * 8 - topk - 1), (0, 0)))
    tall = info.shape[0]
    info = lax.all_to_all(jnp.concatenate([info] * sources, axis=0), BC, 0, 0, tiled=True)
    info = info.reshape(sources, tall, rows)
    ids_all = info[:, :topk]
    seg_all = info[:, topk].reshape(nb, nc, micro, span)
    local = place * mine + jnp.arange(mine)
    hot = jnp.sum((ids_all[:, :, None, :] == local[None, None, :, None]).astype(f32), axis=1)
    hot = hot.reshape(sources, mine, micro, span)
    upper = (jnp.arange(span)[:, None] < jnp.arange(span)[None, :]).astype(bf16)
    within = nn(hot.astype(bf16).reshape(-1, span), upper).reshape(hot.shape)
    totals = jnp.sum(hot, axis=-1)
    earlier = jnp.arange(sources)[:, None] < jnp.arange(sources)[None, :]
    before = jnp.sum(jnp.where(earlier[:, :, None, None], totals[:, None], 0.0), axis=0)
    rank = within + before[..., None]
    room = lax.dynamic_slice(capacity, (place * mine,), (mine,)).astype(f32)
    kept = jnp.where(rank < room[None, :, None, None], hot, 0.0)
    kept = kept.reshape(nb, nc, mine, nt_, cut).transpose(0, 3, 1, 4, 2).reshape(-1, mine)
    ids_rows = ids_all.reshape(nb, nc, topk, nt_, cut).transpose(0, 3, 1, 4, 2).reshape(-1, topk)
    names = jnp.arange(routed)
    marks = jnp.sum((ids_rows[:, :, None] == names).astype(f32), axis=1)
    for e in range(mine):
        marks = marks + jnp.where(names[None, :] == place * mine + e, kept[:, e : e + 1], 0.0)
    piece_rows = nc * cut
    marks = marks.reshape(nb * nt_, piece_rows, routed)
    total_rows = nb * nt_ * piece_rows
    ids_slice = lax.dynamic_slice(expert_ids.reshape(rows, topk), (t * cut, 0), (cut, topk))
    chosen = jnp.sum((ids_slice[:, :, None] == names).astype(f32), axis=1)

    xf = x.astype(f32)
    act1 = (xf * inv_rms(xf) * norm_attn).astype(bf16)
    positions = c * span + jnp.arange(span)
    cosine, sine = angles(positions, hd)
    cosine = jnp.concatenate([cosine] * micro, axis=0)
    sine = jnp.concatenate([sine] * micro, axis=0)
    act1_slice = lax.dynamic_slice(act1, (t * cut, 0), (cut, width))
    own_cols = width // sources

    def columns(v):
        v = gather_t(to_features(v)).reshape(nt_, sources, cut, own_cols)
        return v.transpose(1, 0, 2, 3).reshape(-1, own_cols)

    act1_cols = columns(act1_slice)
    w_or = jnp.concatenate([w_out, pad_cols(w_router, routed)], axis=1)
    dy_slice = lax.dynamic_slice(dy, (t * cut, 0), (cut, width))
    w_qkv, w_or, marks, act1, act1_cols, cosine, sine, dy_tied = after(
        w_qkv, w_or, marks, act1, act1_cols, cosine, sine, dy_slice
    )
    w_or = lax.all_gather(w_or, BC, axis=0, tiled=True)
    dy_own = gather_c(dy_tied)
    n_slab = piece_rows // SLAB
    groups = ((0,), 6 * piece_rows), ((1, 2, 3), 0)
    hidden = mine * w_gate.shape[1]
    gate_w = w_gate.reshape(hidden, width)
    up_w = w_up.reshape(hidden, width)
    down_w = w_down.reshape(hidden, width)
    qkv = nn(act1, w_qkv)
    q_raw = qkv[:, :q_cols].reshape(rows, heads, hd)
    k_raw = qkv[:, q_cols : q_cols + hd]
    q = heads_forward(q_raw, norm_query, cosine[:, None], sine[:, None])
    k = heads_forward(k_raw, norm_key, cosine, sine)
    kv = jnp.concatenate([k, qkv[:, q_cols + hd :].astype(bf16)], axis=1)
    blocks = [
        lax.ppermute(kv, C, [(i, i + s) for i in range(nc - s)]) for s in range(back, 0, -1)
    ]
    window = jnp.stack(blocks + [kv]).reshape(back + 1, micro, span, 2 * hd)
    window = window.transpose(1, 0, 2, 3).reshape(micro, (back + 1) * span, 2 * hd)
    keys, values = window[..., :hd], window[..., hd:]
    seg_seq = lax.dynamic_index_in_dim(seg_all, b, 0, False)
    seg_seq = jnp.pad(seg_seq, ((back, 0), (0, 0), (0, 0)), constant_values=-1)
    seg_win = lax.dynamic_slice(seg_seq, (c, 0, 0), (back + 1, micro, span))
    seg_win = seg_win.transpose(1, 0, 2).reshape(micro, -1)
    seg_own = segment_ids.reshape(micro, span)
    allowed = (seg_own[:, :, None] == seg_win[:, None, :]) & (
        jnp.arange((back + 1) * span)[None, None, :] <= back * span + jnp.arange(span)[None, :, None]
    )
    qg = q.reshape(micro, span, heads, hd).transpose(0, 2, 1, 3)
    qg = qg.reshape(micro, heads * span, hd)
    scores = bdot(qg, keys, 2, 2).reshape(micro, heads, span, -1) * scale
    bias = jnp.where(allowed, 0.0, -1e30)
    side = jnp.where(jnp.arange(hd) < hd // 2, -1.0, 1.0)
    cos_own, sin_own = cosine[:span], sine[:span] * side
    scores = scores + bias[:, None]
    top = jnp.max(scores, axis=-1, keepdims=True)
    weight = jnp.exp(scores - top)
    total = jnp.sum(weight, axis=-1, keepdims=True)
    probs = weight / total
    probs_low = probs.astype(bf16).reshape(micro, heads * span, -1)
    mixed = bdot(probs_low, values, 2, 1).astype(bf16).reshape(micro, heads, span, hd)
    mixed = mixed.transpose(0, 2, 1, 3).reshape(rows, q_cols)
    w_or, dy_own, mixed = after(w_or, dy_own, mixed)
    dy_plane = lax.all_gather(dy_own, T, axis=0, tiled=True)
    out_w = w_or[:, :q_cols]
    router_wide = w_or[:, q_cols:]
    branch = sum_t_permute(nt(mixed, out_w))
    x_slice = lax.dynamic_slice(x, (t * cut, 0), (cut, width)).astype(f32)
    middle = x_slice + branch
    r2 = inv_rms(middle)
    act2 = (middle * r2 * norm_ffn).astype(bf16)
    act2_own = gather_c(act2)
    mixed_later, act2_own, router_wide = after(mixed, act2_own, router_wide)
    mixed_all = lax.all_gather(mixed_later, BC, axis=0, tiled=True)

    places = (
        jnp.arange(routed)[:, None] == place * mine + jnp.arange(hidden)[None, :] // w_gate.shape[1]
    ).astype(bf16)
    consts = (router_wide, places, gate_w, up_w, down_w)

    def experts_on(group, base, near, dys, held):
        pairs = [(side, k) for side in (0, 1) for k in group]
        where = [(b ^ side) * nt_ + (t ^ k) for side, k in pairs]
        where += [(t ^ k) * (dys[0].shape[0] // (nt_ * piece_rows)) for side, k in pairs]
        acts = near + [swap(v) for v in near]
        return expert_pieces(base, jnp.stack(where), acts, dys, marks, consts, held, total_rows)

    half = piece_rows // 2
    from_x, from_y = across(act2_own, 1), across(act2_own, 2)
    held, own_sums = experts_on((0,), 6 * piece_rows, [act2_own], [dy_own, swap(dy_own)], None)
    *held, from_x, from_y, dy_plane = after(*held, from_x, from_y, dy_plane)
    low, high = across(from_x[:half], 2), across(from_y[half:], 1)
    corner = jnp.concatenate([low, high], axis=0)
    held, sums = experts_on((1, 2, 3), 0, [from_x, from_y, corner], [dy_plane, swap(dy_plane)], held)
    ring_sums, corner_sums = sums[0::2], sums[1::2]
    act_all, dy_all, hid_gated, d_gate, d_up = held
    d_in_plane, (hid_later, act2_later) = sum_plane(
        own_sums, ring_sums, corner_sums, (hid_gated, act2)
    )
    blocks, homes = [], []
    for g, start in groups:
        for n, k in enumerate(g):
            for i in range(n_slab):
                first = start // SLAB + i * 2 * len(g) + n
                blocks += [first, first + len(g)]
                homes.append(t ^ k)
    out_near, out_far = out_pieces(hid_later, down_w, blocks, jnp.stack(homes), piece_rows)
    d_in_plane, out_near, out_far, mixed_all = after(d_in_plane, out_near, out_far, mixed_all)
    d_in_got = send_c(d_in_plane)
    out_chip = add_low(out_near, swap(out_far)).reshape(-1, width)
    grad_up = tn(d_up, act_all)
    d_in_got, grad_up, out_chip = after(d_in_got, grad_up, out_chip)

    d_norm, d_branch_slice, d_logits, gain_ffn = turn_back(
        experts, d_in_got, act2_later, middle, dy_slice, chosen, router_wide, norm_ffn[None]
    )
    d_branch = gather_t(d_branch_slice)
    grad_gate = tn(d_gate, act_all)
    d_branch, grad_gate, act2_late, d_logits, out_chip = after(
        d_branch, grad_gate, act2_later, d_logits, out_chip
    )
    out_plane = lax.psum_scatter(out_chip, T, scatter_dimension=0, tiled=True)
    d_branch_cols = to_features(d_branch)
    devices = sources * nt_
    router_part = tn(act2_late, d_logits)[:, :experts]

    d_mixed = nn(d_branch, out_w).astype(bf16)
    d_q, d_window, gain_q = attend_back(
        q.reshape(rows, q_cols), qkv, window, bias, d_mixed, cos_own, sin_own, norm_query[None]
    )
    d_kv = d_window.reshape(micro, back + 1, span, 2 * hd)
    d_kv_own = d_kv[:, back].reshape(rows, 2 * hd).astype(f32)
    for s in range(1, back + 1):
        piece = d_kv[:, back - s].reshape(rows, 2 * hd)
        d_kv_own = d_kv_own + lax.ppermute(piece, C, [(i + s, i) for i in range(nc - s)]).astype(f32)
    d_k_raw, gain_k_rows = heads_back(k_raw, norm_key, cosine, sine, d_kv_own[:, :hd])
    gain_k = jnp.sum(gain_k_rows, axis=0)
    d_qkv = jnp.concatenate([d_q, d_k_raw.astype(bf16), d_kv_own[:, hd:].astype(bf16)], axis=1)
    d_qkv, d_branch_cols = after(d_qkv, d_branch_cols)
    late = lax.all_gather(d_qkv, BC, axis=0, tiled=True)
    d_act1_part = nt(d_qkv, w_qkv)
    gain_attn = jnp.sum(d_act1_part * (xf * inv_rms(xf)), axis=0)
    d_act1 = sum_t_permute(d_act1_part)
    d_norm1, _ = norm_back(x_slice, inv_rms(x_slice), norm_attn, d_act1)

    pieces = [v.reshape(devices, -1) for v in (router_part, gain_attn, gain_ffn, gain_q, gain_k)]
    sizes = [v.shape[1] for v in pieces]
    flat = jnp.concatenate(pieces, axis=1).astype(bf16)
    flat = lax.all_to_all(pad_cols(flat, -(-flat.shape[1] // 128) * 128), ALL, 0, 0, tiled=True)
    flat = jnp.sum(flat.astype(f32), axis=0, keepdims=True)
    lines = -(-flat.shape[1] // width)
    flat = pad_cols(flat, lines * width).reshape(lines, width)
    flat = jnp.pad(flat, ((0, -lines % 16), (0, 0)))
    final = jnp.concatenate([d_norm + d_norm1, flat], axis=0).astype(bf16)
    final, out_plane, dy_all, mixed_all = after(final, out_plane, dy_all, mixed_all)
    out_sum = sum_c_permute(out_plane)
    final = gather_t(final).astype(f32).reshape(nt_, -1, width)
    grad_in = final[:, :cut].reshape(rows, width) + dy.astype(f32)
    grad_qkv = tn(act1_cols, late)
    hidden_out, grad_qkv = after(gather_t((branch + out_sum).astype(bf16)), grad_qkv)
    hidden_out = hidden_out.astype(f32) + xf
    flat = final[:, cut : cut + lines].reshape(nt_, lines * width)
    gains, start = [], 0
    for size in sizes:
        gains.append(flat[:, start : start + size].reshape(-1))
        start += size
    grad_router = gains.pop(0).reshape(-1, experts)
    grad_down = tn(hid_gated, dy_all)
    grad_out_w = tn(d_branch_cols, mixed_all)
    shape = hidden_in.shape
    return (
        hidden_out.reshape(shape),
        grad_in.reshape(shape),
        gains[0],
        gains[1],
        gains[2],
        gains[3],
        grad_qkv[:, :q_cols],
        grad_qkv[:, q_cols : q_cols + hd],
        grad_qkv[:, q_cols + hd :],
        grad_out_w,
        grad_router,
        grad_gate.reshape(w_gate.shape),
        grad_up.reshape(w_up.shape),
        grad_down.reshape(w_down.shape),
    )


def solution(mesh):
    rows = P(None, B, C, None)
    ids = P(None, B, C)
    whole = P()
    matrix = P(BC, T)
    router = P(BC, None)
    expert = P(BC, T, None)
    vector = P(BC)
    in_specs = (rows, ids, rows) + (whole,) * 5 + (matrix,) * 4 + (router,) + (expert,) * 3 + (rows,)
    out_specs = (rows, rows) + (vector,) * 4 + (matrix,) * 4 + (router,) + (expert,) * 3
    return jax.shard_map(body, mesh=mesh, in_specs=in_specs, out_specs=out_specs, check_vma=False)
```

```python
import functools

import jax
import jax.numpy as jnp
from jax import lax
from jax.experimental import pallas as pl
from jax.experimental.pallas import tpu as pltpu
from jax.sharding import PartitionSpec as P

B, C, T = "batch", "ctx", "tensor"
BC = (B, C)
ALL = (B, C, T)
f32 = jnp.float32
bf16 = jnp.bfloat16
EPS = 1e-06


def dot(a, b, ca, cb):
    return lax.dot_general(a, b, (((ca,), (cb,)), ((), ())), preferred_element_type=f32)


def nn(a, b):
    return dot(a, b, 1, 0)


def nt(a, b):
    return dot(a, b, 1, 1)


def tn(a, b):
    return dot(a, b, 0, 0)


def bdot(a, b, ca, cb):
    return lax.dot_general(a, b, (((ca,), (cb,)), ((0,), (0,))), preferred_element_type=f32)


def after(*values):
    return lax.optimization_barrier(values)


def pad_cols(v, width):
    return jnp.pad(v, ((0, 0), (0, width - v.shape[1])))


def inv_rms(v):
    return lax.rsqrt(jnp.mean(v * v, axis=-1, keepdims=True) + EPS)


def turn(v):
    half = v.shape[-1] // 2
    return jnp.concatenate([-v[..., half:], v[..., :half]], axis=-1)


def angles(positions, width):
    half = width // 2
    frequency = jnp.power(1000000.0, -(2.0 * jnp.arange(half, dtype=f32)) / width)
    phases = positions.astype(f32)[:, None] * frequency[None, :]
    phases = jnp.concatenate([phases, phases], axis=-1)
    return jnp.cos(phases), jnp.sin(phases)


def norm_back(v, r, gain, grad):
    scaled = gain * grad
    grad_v = r * scaled - v * (r * r * r) * jnp.mean(v * scaled, axis=-1, keepdims=True)
    return grad_v, grad * v * r


def heads_forward(raw, gain, cosine, sine):
    v = raw * inv_rms(raw) * gain
    return (v * cosine + turn(v) * sine).astype(bf16)


def heads_back(raw, gain, cosine, sine, grad):
    grad = grad * cosine - turn(grad) * sine
    return norm_back(raw, inv_rms(raw), gain, grad)


def gather_t(v):
    count = lax.axis_size(T)
    return lax.all_to_all(jnp.concatenate([v] * count, axis=0), T, 0, 0, tiled=True)


def sum_t(v):
    count = lax.axis_size(T)
    got = lax.all_to_all(v.astype(bf16), T, 0, 0, tiled=True)
    got = got.reshape(count, v.shape[0] // count, v.shape[1])
    return jnp.sum(got.astype(f32), axis=0)


def swap(v):
    return lax.ppermute(v, B, [(0, 1), (1, 0)])


def across(v, k):
    return lax.ppermute(v, T, [(i, i ^ k) for i in range(lax.axis_size(T))])


def add_low(*parts):
    total = parts[0].astype(f32)
    for part in parts[1:]:
        total = total + part.astype(f32)
    return total.astype(bf16)


def gather_c(v):
    count = lax.axis_size(C)
    return lax.all_to_all(jnp.concatenate([v] * count, axis=0), C, 0, 0, tiled=True)


def spread_plane(own):
    half = own.shape[0] // 2
    from_x, from_y = across(own, 1), across(own, 2)
    low, high = across(from_x[:half], 2), across(from_y[half:], 1)
    return [own, from_x, from_y, jnp.concatenate([low, high], axis=0)]


def sum_plane(own, ring, corner, held=()):
    diagonal = add_low(corner[0][0], swap(corner[1])[0])
    half = diagonal.shape[0] // 2
    ring_far = swap(ring[1])
    east = add_low(ring[0][0, :half], ring_far[0, :half])
    north = add_low(ring[0][1, half:], ring_far[1, half:])
    diagonal, east, north = after(diagonal, east, north)
    from_x, from_y = across(diagonal[:half], 1), across(diagonal[half:], 2)
    east_top, north_low = across(east, 1), across(north, 2)
    own_far = swap(own[1])
    east = add_low(ring[0][0, half:], ring_far[0, half:], from_y)
    north = add_low(ring[0][1, :half], ring_far[1, :half], from_x)
    east, north, *held = after(east, north, *held)
    east_low, north_top = across(east, 1), across(north, 2)
    top = add_low(own[0][0, :half], own_far[0, :half], east_top, north_top)
    low = add_low(own[0][0, half:], own_far[0, half:], east_low, north_low)
    return jnp.concatenate([top, low], axis=0), held


def to_features(v):
    return lax.all_to_all(v, BC, 1, 0, tiled=True)


def send_c(plane):
    count = lax.axis_size(C)
    got = lax.all_to_all(plane, C, 0, 0, tiled=True)
    return got.reshape(count, plane.shape[0] // count, plane.shape[1])


SLAB = 256


def sum_c_permute(plane):
    count = lax.axis_size(C)
    cut = plane.shape[0] // count
    c = lax.axis_index(C)
    block = lambda k: lax.dynamic_slice(plane, (((c + k) % count) * cut, 0), (cut, plane.shape[1]))
    total = block(0).astype(f32)
    for k in range(1, count):
        got = lax.ppermute(block(k), C, [(i, (i + k) % count) for i in range(count)])
        total = total + got.astype(f32)
    return total


def expert_kernel(count, first, where_ref, *refs):
    acts, dys, marks = refs[:count], refs[count : count + 2], refs[count + 2 : 2 * count + 2]
    router_ref, place_ref = refs[2 * count + 2 : 2 * count + 4]
    weights_hbm = refs[2 * count + 4 : 2 * count + 7]
    act_b, dy_b, hid_b, dg_b, du_b, din_b, mark_b = refs[-13:-6]
    gate_w, up_w, down_w = refs[-6:-3]
    in_sem, w_sem, out_sem = refs[-3:]
    sizes = [min(2, count // 2)] + [1] * (count // 2 > 2)
    outs = refs[-18 - 2 * len(sizes) : -13]
    act_all, dy_all, hid_all, dg_all, du_all = outs[:5]
    given, low_p = [], 0
    for size, to in zip(sizes * 2, outs[5:]):
        given.append((low_p, size, to))
        low_p += size
    i = pl.program_id(0)
    width = act_b.shape[2]
    hidden = gate_w.shape[0]
    src = pl.ds(pl.multiple_of(i * SLAB, SLAB), SLAB)
    base = first + i * count * SLAB
    stored = ((act_b, act_all), (dy_b, dy_all), (hid_b, hid_all), (dg_b, dg_all), (du_b, du_all))
    weights = [
        pltpu.make_async_copy(v, w, w_sem.at[k])
        for k, (v, w) in enumerate(zip(weights_hbm, (gate_w, up_w, down_w)))
    ]

    piece = pl.num_programs(0) * SLAB

    def load(k, p):
        if k == 0:
            return pltpu.make_async_copy(acts[p].at[src], act_b.at[p], in_sem.at[0, p])
        rows = pl.ds(pl.multiple_of(where_ref[count + p] * piece + i * SLAB, SLAB), SLAB)
        return pltpu.make_async_copy(dys[p // (count // 2)].at[rows], dy_b.at[p], in_sem.at[1, p])

    def stores(p):
        rows = pl.ds(pl.multiple_of(base + p * SLAB, SLAB), SLAB)
        return [
            pltpu.make_async_copy(v.at[p], to.at[rows], out_sem.at[k, p])
            for k, (v, to) in enumerate(stored)
        ]

    def give(p, place, to):
        return pltpu.make_async_copy(din_b.at[p], to.at[place, src], out_sem.at[5, p])

    load(0, 0).start()

    @pl.when(i == 0)
    def _():
        weights[0].start()
        weights[1].start()

    load(1, 0).start()

    @pl.when(i == 0)
    def _():
        weights[2].start()

    for p in range(count):
        mark_b[p] = marks[p][0]

    @pl.when(i == 0)
    def _():
        weights[0].wait()
        weights[1].wait()

    def one(p, carry):
        for k, buffer in enumerate((act_b, dy_b)):
            pltpu.make_async_copy(acts[0].at[src], buffer.at[p], in_sem.at[k, p]).wait()
        for q in range(1, count):

            @pl.when(p == q - 1)
            def _(q=q):
                load(0, q).start()
                load(1, q).start()

        act = act_b[p]
        mark = mark_b[p]
        logits = nn(act, router_ref[...])
        top = jnp.max(jnp.where(mark > 0.5, logits, -1e30), axis=1, keepdims=True)
        parts = jnp.where(mark > 0.5, jnp.exp(logits - top), 0.0)
        parts = parts / jnp.sum(parts, axis=1, keepdims=True)
        gates = jnp.where(mark > 1.5, parts, 0.0)
        high = gates.astype(bf16)
        low = (gates - high.astype(f32)).astype(bf16)

        @pl.when((p == 0) & (i == 0))
        def _():
            weights[2].wait()

        place = place_ref[...]
        wide = nn(high, place) + nn(low, place)
        gate = nt(act, gate_w[...])
        up = nt(act, up_w[...])
        dyw = nt(dy_b[p], down_w[...])
        sig = 0.5 * jnp.tanh(0.5 * gate) + 0.5
        silu = gate * sig
        hid = silu * up
        hid_b[p] = (wide * hid).astype(bf16)
        share = nt((hid * dyw).astype(bf16), place)
        d_hid = wide * dyw
        dg_b[p] = (d_hid * up * (sig + silu * (1.0 - sig))).astype(bf16)
        du_b[p] = (d_hid * silu).astype(bf16)
        din_b[p, :, width:] = jnp.where(mark > 1.5, share, 0.0).astype(bf16)
        for w in range(0, width, 512):
            cols = slice(w, w + 512)
            total = nn(dg_b[p], gate_w[:, cols]) + nn(du_b[p], up_w[:, cols])
            din_b[p, :, cols] = total.astype(bf16)
        for copy in stores(p):
            copy.start()

        for low_p, size, to in given:

            @pl.when((p >= low_p) & (p < low_p + size))
            def _(low_p=low_p, to=to):
                give(p, p - low_p, to).start()

        return carry

    lax.fori_loop(0, count, one, 0)
    for p in range(count):
        for copy in stores(p):
            copy.wait()
        for low_p, size, to in given:
            if low_p <= p < low_p + size:
                give(p, p - low_p, to).wait()


def expert_pieces(first, where, acts, dys, marks, consts, held, total_rows):
    count = len(acts)
    rows, width = acts[0].shape
    hidden = consts[2].shape[0]
    routed = consts[0].shape[1]
    left = pl.BlockSpec(memory_space=pl.ANY)
    in_specs = [left] * (count + 2)
    in_specs += [
        pl.BlockSpec((1, SLAB, routed), lambda i, w, p=p: (w[p], i, 0)) for p in range(count)
    ]
    in_specs += [
        pl.BlockSpec(v.shape, lambda i, w: (0, 0), pipeline_mode=pl.Buffered(1)) for v in consts[:2]
    ]
    in_specs += [left] * 3
    out_shape = [jax.ShapeDtypeStruct((total_rows, width), bf16)] * 2
    out_shape += [jax.ShapeDtypeStruct((total_rows, hidden), bf16)] * 3
    sizes = [min(2, count // 2)] + [1] * (count // 2 > 2)
    out_shape += [jax.ShapeDtypeStruct((size, rows, width + routed), bf16) for size in sizes * 2]
    args = [where, *acts, *dys, *([marks] * count), *consts]
    aliases = {}
    if held is not None:
        for k, v in enumerate(held):
            aliases[len(args)] = k
            args.append(v)
            in_specs.append(left)
    outs = pl.pallas_call(
        functools.partial(expert_kernel, count, first),
        grid_spec=pltpu.PrefetchScalarGridSpec(
            num_scalar_prefetch=1,
            grid=(rows // SLAB,),
            in_specs=in_specs,
            out_specs=[left] * len(out_shape),
            scratch_shapes=[pltpu.VMEM((count, SLAB, width), bf16)] * 2
            + [pltpu.VMEM((count, SLAB, hidden), bf16)] * 3
            + [pltpu.VMEM((count, SLAB, width + routed), bf16)]
            + [pltpu.VMEM((count, SLAB, routed), f32)]
            + [pltpu.VMEM((hidden, width), bf16)] * 3
            + [pltpu.SemaphoreType.DMA((2, count))]
            + [pltpu.SemaphoreType.DMA((3,))]
            + [pltpu.SemaphoreType.DMA((6, count))],
        ),
        out_shape=out_shape,
        input_output_aliases=aliases,
        compiler_params=pltpu.CompilerParams(vmem_limit_bytes=56 << 20),
        cost_estimate=pl.CostEstimate(flops=1000, bytes_accessed=1000, transcendentals=0),
    )(*args)
    return outs[:5], outs[5:]


def attend_back_kernel(heads, scale, q_ref, raw_ref, kv_ref, bias_ref, dm_ref, cos_ref, sin_ref, gain_ref, dq_ref, dkv_ref, gq_ref, rows_q, rows_m, rows_p, rows_s):
    span = q_ref.shape[0]
    hd = gain_ref.shape[1]
    keys, values = kv_ref[0, :, :hd], kv_ref[0, :, hd:]
    bias = bias_ref[0]
    cosine, sine = cos_ref[...], sin_ref[...]
    gain = gain_ref[...]

    @pl.when(pl.program_id(0) == 0)
    def _():
        gq_ref[...] = jnp.zeros_like(gq_ref)

    total = jnp.zeros((1, hd), f32)
    for h in range(heads):
        cols = slice(h * hd, (h + 1) * hd)
        lines = slice(h * span, (h + 1) * span)
        q = q_ref[:, cols]
        dm = dm_ref[:, cols]
        rows_q[lines, :] = q
        rows_m[lines, :] = dm
        scores = nt(q, keys) * scale + bias
        weight = jnp.exp(scores - jnp.max(scores, axis=1, keepdims=True))
        probs = weight / jnp.sum(weight, axis=1, keepdims=True)
        d_probs = nt(dm, values)
        d_scores = probs * (d_probs - jnp.sum(probs * d_probs, axis=1, keepdims=True))
        low = d_scores.astype(bf16)
        rows_p[lines, :] = probs.astype(bf16)
        rows_s[lines, :] = low
        d_q = nn(low, keys) * scale
        grad = d_q * cosine - pltpu.roll(d_q, hd // 2, 1) * sine
        raw = raw_ref[:, cols]
        d_raw, gain_rows = norm_back(raw, inv_rms(raw), gain, grad)
        dq_ref[:, cols] = d_raw.astype(bf16)
        total = total + jnp.sum(gain_rows, axis=0, keepdims=True)
    gq_ref[...] += total
    dkv_ref[0, :, :hd] = (tn(rows_s[...], rows_q[...]) * scale).astype(bf16)
    dkv_ref[0, :, hd:] = tn(rows_p[...], rows_m[...]).astype(bf16)


def attend_back(q, qkv, window, bias, d_mixed, cosine, sine, gain):
    micro, reach, pair = window.shape
    hd = pair // 2
    span, q_cols = q.shape[0] // micro, q.shape[1]
    heads = q_cols // hd
    row = lambda m: (m, 0)
    flat = lambda m: (0, 0)
    deep = lambda m: (m, 0, 0)
    return pl.pallas_call(
        functools.partial(attend_back_kernel, heads, hd ** (-0.5)),
        grid=(micro,),
        in_specs=[
            pl.BlockSpec((span, q_cols), row),
            pl.BlockSpec((span, q_cols), row),
            pl.BlockSpec((1, reach, pair), deep),
            pl.BlockSpec((1, span, reach), deep),
            pl.BlockSpec((span, q_cols), row),
            pl.BlockSpec((span, hd), flat),
            pl.BlockSpec((span, hd), flat),
            pl.BlockSpec((1, hd), flat),
        ],
        out_specs=[
            pl.BlockSpec((span, q_cols), row),
            pl.BlockSpec((1, reach, pair), deep),
            pl.BlockSpec((1, hd), flat),
        ],
        out_shape=[
            jax.ShapeDtypeStruct(q.shape, bf16),
            jax.ShapeDtypeStruct(window.shape, bf16),
            jax.ShapeDtypeStruct((1, hd), f32),
        ],
        scratch_shapes=[pltpu.VMEM((heads * span, hd), bf16)] * 2
        + [pltpu.VMEM((heads * span, reach), bf16)] * 2,
        compiler_params=pltpu.CompilerParams(vmem_limit_bytes=32 << 20),
        cost_estimate=pl.CostEstimate(
            flops=10 * micro * heads * span * reach * hd,
            bytes_accessed=10 * micro * span * q_cols,
            transcendentals=micro * heads * span * reach,
        ),
    )(q, qkv, window, bias, d_mixed, cosine, sine, gain)


def turn_back_kernel(experts, got_ref, act_ref, mid_ref, dy_ref, chosen_ref, router_ref, gain_ref, dn_ref, low_ref, dl_ref, gain_out):
    width = mid_ref.shape[1]
    total = got_ref[0].astype(f32)
    for k in range(1, got_ref.shape[0]):
        total = total + got_ref[k].astype(f32)
    d_gates = total[:, width:]
    router = router_ref[...]
    chosen = chosen_ref[...]
    logits = nn(act_ref[...], router)
    real = lax.broadcasted_iota(jnp.int32, logits.shape, 1) < experts
    logits = jnp.where(real, logits, -1e30)
    weight = jnp.exp(logits - jnp.max(logits, axis=1, keepdims=True))
    probs = weight / jnp.sum(weight, axis=1, keepdims=True)
    picked = probs * chosen
    picked_sum = jnp.sum(picked, axis=1, keepdims=True)
    lean = jnp.sum(d_gates * picked / picked_sum, axis=1, keepdims=True)
    c_grad = chosen * (d_gates - lean) / picked_sum
    d_logits = probs * (c_grad - jnp.sum(probs * c_grad, axis=1, keepdims=True))
    d_logits = jnp.where(real, d_logits, 0.0).astype(bf16)
    dl_ref[...] = d_logits
    d_act = total[:, :width] + nt(d_logits, router)
    middle = mid_ref[...]
    d_norm, gain_rows = norm_back(middle, inv_rms(middle), gain_ref[...], d_act)
    dn_ref[...] = d_norm
    low_ref[...] = (dy_ref[...].astype(f32) + d_norm).astype(bf16)
    gain_out[...] = jnp.sum(gain_rows, axis=0, keepdims=True)


def turn_back(experts, got, act2, middle, dy_slice, chosen, router, gain):
    cut, width = middle.shape
    routed = router.shape[1]
    return pl.pallas_call(
        functools.partial(turn_back_kernel, experts),
        out_shape=[
            jax.ShapeDtypeStruct((cut, width), f32),
            jax.ShapeDtypeStruct((cut, width), bf16),
            jax.ShapeDtypeStruct((cut, routed), bf16),
            jax.ShapeDtypeStruct((1, width), f32),
        ],
        compiler_params=pltpu.CompilerParams(vmem_limit_bytes=32 << 20),
        cost_estimate=pl.CostEstimate(
            flops=4 * cut * width * routed, bytes_accessed=20 * cut * width, transcendentals=cut * routed
        ),
    )(got, act2, middle, dy_slice, chosen, router, gain)


def out_kernel(where_ref, hid_ref, down_ref, near_ref, far_ref):
    p = pl.program_id(0)
    value = nn(hid_ref[...], down_ref[...]).astype(bf16)

    @pl.when(p % 2 == 0)
    def _():
        near_ref[0] = value

    @pl.when(p % 2 == 1)
    def _():
        far_ref[0] = value


def out_pieces(hid, down, blocks, homes, piece_rows):
    hidden, width = down.shape
    count = lax.axis_size(T)
    n_slab = piece_rows // SLAB
    where = jnp.concatenate([jnp.asarray(blocks, jnp.int32), homes])
    n = len(blocks)
    home = lambda p, w: (w[n + p // 2], (p // 2) % n_slab, 0)
    return pl.pallas_call(
        out_kernel,
        grid_spec=pltpu.PrefetchScalarGridSpec(
            num_scalar_prefetch=1,
            grid=(n,),
            in_specs=[
                pl.BlockSpec((SLAB, hidden), lambda p, w: (w[p], 0)),
                pl.BlockSpec((hidden, width), lambda p, w: (0, 0), pipeline_mode=pl.Buffered(1)),
            ],
            out_specs=[pl.BlockSpec((1, SLAB, width), home)] * 2,
        ),
        out_shape=[jax.ShapeDtypeStruct((count, piece_rows, width), bf16)] * 2,
        compiler_params=pltpu.CompilerParams(vmem_limit_bytes=32 << 20),
        cost_estimate=pl.CostEstimate(flops=1000, bytes_accessed=1000, transcendentals=0),
    )(where, hid, down)


def sum_t_permute(v):
    count = lax.axis_size(T)
    cut = v.shape[0] // count
    t = lax.axis_index(T)
    low = v.astype(bf16)
    block = lambda k: lax.dynamic_slice(low, ((t ^ k) * cut, 0), (cut, v.shape[1]))
    total = block(0).astype(f32)
    for k in range(1, count):
        total = total + across(block(k), k).astype(f32)
    return total


def body(
    hidden_in,
    segment_ids,
    expert_ids,
    capacity,
    norm_attn,
    norm_ffn,
    norm_query,
    norm_key,
    w_query,
    w_key,
    w_value,
    w_out,
    w_router,
    w_gate,
    w_up,
    w_down,
    grad_out,
):
    micro, _, span, width = hidden_in.shape
    rows = micro * span
    hd = norm_query.shape[0]
    topk = expert_ids.shape[3]
    experts = w_router.shape[1]
    mine = w_gate.shape[0]
    nb, nc, nt_ = lax.axis_size(B), lax.axis_size(C), lax.axis_size(T)
    sources = nb * nc
    cut = rows // nt_
    b, c, t = lax.axis_index(B), lax.axis_index(C), lax.axis_index(T)
    place = b * nc + c
    seq = span * nc
    back = (seq // 2 - 1 + span - 1) // span
    heads = w_query.shape[1] // hd
    q_cols = heads * hd
    scale = hd ** (-0.5)
    routed = -(-experts // 128) * 128

    x = hidden_in.reshape(rows, width)
    dy = grad_out.reshape(rows, width)

    w_qkv = lax.all_gather(
        jnp.concatenate([w_query, w_key, w_value], axis=1), BC, axis=0, tiled=True
    )
    ids_own = expert_ids.reshape(rows, topk).T
    info = jnp.concatenate([ids_own, segment_ids.reshape(1, rows)], axis=0)
    info = jnp.pad(info, ((0, -(-(topk + 1) // 8) * 8 - topk - 1), (0, 0)))
    tall = info.shape[0]
    info = lax.all_to_all(jnp.concatenate([info] * sources, axis=0), BC, 0, 0, tiled=True)
    info = info.reshape(sources, tall, rows)
    ids_all = info[:, :topk]
    seg_all = info[:, topk].reshape(nb, nc, micro, span)
    local = place * mine + jnp.arange(mine)
    hot = jnp.sum((ids_all[:, :, None, :] == local[None, None, :, None]).astype(f32), axis=1)
    hot = hot.reshape(sources, mine, micro, span)
    upper = (jnp.arange(span)[:, None] < jnp.arange(span)[None, :]).astype(bf16)
    within = nn(hot.astype(bf16).reshape(-1, span), upper).reshape(hot.shape)
    totals = jnp.sum(hot, axis=-1)
    earlier = jnp.arange(sources)[:, None] < jnp.arange(sources)[None, :]
    before = jnp.sum(jnp.where(earlier[:, :, None, None], totals[:, None], 0.0), axis=0)
    rank = within + before[..., None]
    room = lax.dynamic_slice(capacity, (place * mine,), (mine,)).astype(f32)
    kept = jnp.where(rank < room[None, :, None, None], hot, 0.0)
    kept = kept.reshape(nb, nc, mine, nt_, cut).transpose(0, 3, 1, 4, 2).reshape(-1, mine)
    ids_rows = ids_all.reshape(nb, nc, topk, nt_, cut).transpose(0, 3, 1, 4, 2).reshape(-1, topk)
    names = jnp.arange(routed)
    marks = jnp.sum((ids_rows[:, :, None] == names).astype(f32), axis=1)
    for e in range(mine):
        marks = marks + jnp.where(names[None, :] == place * mine + e, kept[:, e : e + 1], 0.0)
    piece_rows = nc * cut
    marks = marks.reshape(nb * nt_, piece_rows, routed)
    total_rows = nb * nt_ * piece_rows
    ids_slice = lax.dynamic_slice(expert_ids.reshape(rows, topk), (t * cut, 0), (cut, topk))
    chosen = jnp.sum((ids_slice[:, :, None] == names).astype(f32), axis=1)

    xf = x.astype(f32)
    act1 = (xf * inv_rms(xf) * norm_attn).astype(bf16)
    positions = c * span + jnp.arange(span)
    cosine, sine = angles(positions, hd)
    cosine = jnp.concatenate([cosine] * micro, axis=0)
    sine = jnp.concatenate([sine] * micro, axis=0)
    act1_slice = lax.dynamic_slice(act1, (t * cut, 0), (cut, width))
    own_cols = width // sources

    def columns(v):
        v = gather_t(v).reshape(nt_, sources, cut, own_cols)
        return v.transpose(1, 0, 2, 3).reshape(-1, own_cols)

    act1_cols = columns(to_features(act1_slice))
    w_or = jnp.concatenate([w_out, pad_cols(w_router, routed)], axis=1)
    dy_slice = lax.dynamic_slice(dy, (t * cut, 0), (cut, width))
    w_qkv, w_or, marks, act1, act1_cols, cosine, sine, dy_tied = after(
        w_qkv, w_or, marks, act1, act1_cols, cosine, sine, dy_slice
    )
    w_or = lax.all_gather(w_or, BC, axis=0, tiled=True)
    dy_own = gather_c(dy_tied)
    n_slab = piece_rows // SLAB
    groups = ((0,), 6 * piece_rows), ((1, 2, 3), 0)
    hidden = mine * w_gate.shape[1]
    gate_w = w_gate.reshape(hidden, width)
    up_w = w_up.reshape(hidden, width)
    down_w = w_down.reshape(hidden, width)
    qkv = nn(act1, w_qkv)
    q_raw = qkv[:, :q_cols].reshape(rows, heads, hd)
    k_raw = qkv[:, q_cols : q_cols + hd]
    q = heads_forward(q_raw, norm_query, cosine[:, None], sine[:, None])
    k = heads_forward(k_raw, norm_key, cosine, sine)
    kv = jnp.concatenate([k, qkv[:, q_cols + hd :].astype(bf16)], axis=1)
    blocks = [
        lax.ppermute(kv, C, [(i, i + s) for i in range(nc - s)]) for s in range(back, 0, -1)
    ]
    window = jnp.stack(blocks + [kv]).reshape(back + 1, micro, span, 2 * hd)
    window = window.transpose(1, 0, 2, 3).reshape(micro, (back + 1) * span, 2 * hd)
    keys, values = window[..., :hd], window[..., hd:]
    seg_seq = lax.dynamic_index_in_dim(seg_all, b, 0, False)
    seg_seq = jnp.pad(seg_seq, ((back, 0), (0, 0), (0, 0)), constant_values=-1)
    seg_win = lax.dynamic_slice(seg_seq, (c, 0, 0), (back + 1, micro, span))
    seg_win = seg_win.transpose(1, 0, 2).reshape(micro, -1)
    seg_own = segment_ids.reshape(micro, span)
    allowed = (seg_own[:, :, None] == seg_win[:, None, :]) & (
        jnp.arange((back + 1) * span)[None, None, :] <= back * span + jnp.arange(span)[None, :, None]
    )
    qg = q.reshape(micro, span, heads, hd).transpose(0, 2, 1, 3)
    qg = qg.reshape(micro, heads * span, hd)
    scores = bdot(qg, keys, 2, 2).reshape(micro, heads, span, -1) * scale
    bias = jnp.where(allowed, 0.0, -1e30)
    side = jnp.where(jnp.arange(hd) < hd // 2, -1.0, 1.0)
    cos_own, sin_own = cosine[:span], sine[:span] * side
    scores = scores + bias[:, None]
    top = jnp.max(scores, axis=-1, keepdims=True)
    weight = jnp.exp(scores - top)
    total = jnp.sum(weight, axis=-1, keepdims=True)
    probs = weight / total
    probs_low = probs.astype(bf16).reshape(micro, heads * span, -1)
    mixed = bdot(probs_low, values, 2, 1).astype(bf16).reshape(micro, heads, span, hd)
    mixed = mixed.transpose(0, 2, 1, 3).reshape(rows, q_cols)
    w_or, dy_own, mixed = after(w_or, dy_own, mixed)
    dy_plane = lax.all_gather(dy_own, T, axis=0, tiled=True)
    out_w = w_or[:, :q_cols]
    router_wide = w_or[:, q_cols:]
    branch = sum_t_permute(nt(mixed, out_w))
    x_slice = lax.dynamic_slice(x, (t * cut, 0), (cut, width)).astype(f32)
    middle = x_slice + branch
    r2 = inv_rms(middle)
    act2 = (middle * r2 * norm_ffn).astype(bf16)
    act2_own = gather_c(act2)
    mixed_later, act2_own, router_wide = after(mixed, act2_own, router_wide)
    mixed_all = lax.all_gather(mixed_later, BC, axis=0, tiled=True)

    places = (
        jnp.arange(routed)[:, None] == place * mine + jnp.arange(hidden)[None, :] // w_gate.shape[1]
    ).astype(bf16)
    consts = (router_wide, places, gate_w, up_w, down_w)

    def experts_on(group, base, near, dys, held):
        pairs = [(side, k) for side in (0, 1) for k in group]
        where = [(b ^ side) * nt_ + (t ^ k) for side, k in pairs]
        where += [(t ^ k) * (dys[0].shape[0] // (nt_ * piece_rows)) for side, k in pairs]
        acts = near + [swap(v) for v in near]
        return expert_pieces(base, jnp.stack(where), acts, dys, marks, consts, held, total_rows)

    half = piece_rows // 2
    from_x, from_y = across(act2_own, 1), across(act2_own, 2)
    held, own_sums = experts_on((0,), 6 * piece_rows, [act2_own], [dy_own, swap(dy_own)], None)
    *held, from_x, from_y, dy_plane = after(*held, from_x, from_y, dy_plane)
    low, high = across(from_x[:half], 2), across(from_y[half:], 1)
    corner = jnp.concatenate([low, high], axis=0)
    held, sums = experts_on((1, 2, 3), 0, [from_x, from_y, corner], [dy_plane, swap(dy_plane)], held)
    ring_sums, corner_sums = sums[0::2], sums[1::2]
    act_all, dy_all, hid_gated, d_gate, d_up = held
    d_in_plane, (hid_later, act2_later) = sum_plane(
        own_sums, ring_sums, corner_sums, (hid_gated, act2)
    )
    blocks, homes = [], []
    for g, start in groups:
        for n, k in enumerate(g):
            for i in range(n_slab):
                first = start // SLAB + i * 2 * len(g) + n
                blocks += [first, first + len(g)]
                homes.append(t ^ k)
    out_near, out_far = out_pieces(hid_later, down_w, blocks, jnp.stack(homes), piece_rows)
    d_in_plane, out_near, out_far, mixed_all = after(d_in_plane, out_near, out_far, mixed_all)
    d_in_got = send_c(d_in_plane)
    out_chip = add_low(out_near, swap(out_far)).reshape(-1, width)
    grad_up = tn(d_up, act_all)
    d_in_got, grad_up, out_chip = after(d_in_got, grad_up, out_chip)

    d_norm, d_branch_slice, d_logits, gain_ffn = turn_back(
        experts, d_in_got, act2_later, middle, dy_slice, chosen, router_wide, norm_ffn[None]
    )
    d_branch = gather_t(d_branch_slice)
    grad_gate = tn(d_gate, act_all)
    d_branch, grad_gate, act2_late, d_logits, out_chip, d_branch_slice = after(
        d_branch, grad_gate, act2_later, d_logits, out_chip, d_branch_slice
    )
    out_plane = lax.psum_scatter(out_chip, T, scatter_dimension=0, tiled=True)
    d_branch_part = to_features(d_branch_slice)
    devices = sources * nt_
    router_part = tn(act2_late, d_logits)[:, :experts]

    d_mixed = nn(d_branch, out_w).astype(bf16)
    d_mixed, d_branch_part = after(d_mixed, d_branch_part)
    d_branch_cols = columns(d_branch_part)
    d_q, d_window, gain_q = attend_back(
        q.reshape(rows, q_cols), qkv, window, bias, d_mixed, cos_own, sin_own, norm_query[None]
    )
    d_kv = d_window.reshape(micro, back + 1, span, 2 * hd)
    d_kv_own = d_kv[:, back].reshape(rows, 2 * hd).astype(f32)
    for s in range(1, back + 1):
        piece = d_kv[:, back - s].reshape(rows, 2 * hd)
        d_kv_own = d_kv_own + lax.ppermute(piece, C, [(i + s, i) for i in range(nc - s)]).astype(f32)
    d_k_raw, gain_k_rows = heads_back(k_raw, norm_key, cosine, sine, d_kv_own[:, :hd])
    gain_k = jnp.sum(gain_k_rows, axis=0)
    d_qkv = jnp.concatenate([d_q, d_k_raw.astype(bf16), d_kv_own[:, hd:].astype(bf16)], axis=1)
    late = lax.all_gather(d_qkv, BC, axis=0, tiled=True)
    d_act1_part = nt(d_qkv, w_qkv)
    gain_attn = jnp.sum(d_act1_part * (xf * inv_rms(xf)), axis=0)
    d_act1, d_branch_cols = after(sum_t_permute(d_act1_part), d_branch_cols)
    d_norm1, _ = norm_back(x_slice, inv_rms(x_slice), norm_attn, d_act1)

    pieces = [v.reshape(devices, -1) for v in (router_part, gain_attn, gain_ffn, gain_q, gain_k)]
    sizes = [v.shape[1] for v in pieces]
    flat = jnp.concatenate(pieces, axis=1).astype(bf16)
    flat = lax.all_to_all(pad_cols(flat, -(-flat.shape[1] // 128) * 128), ALL, 0, 0, tiled=True)
    flat = jnp.sum(flat.astype(f32), axis=0, keepdims=True)
    lines = -(-flat.shape[1] // width)
    flat = pad_cols(flat, lines * width).reshape(lines, width)
    flat = jnp.pad(flat, ((0, -lines % 16), (0, 0)))
    final = jnp.concatenate([d_norm + d_norm1, flat], axis=0).astype(bf16)
    final, out_plane, dy_all, mixed_all = after(final, out_plane, dy_all, mixed_all)
    out_sum = sum_c_permute(out_plane)
    final = gather_t(final).astype(f32).reshape(nt_, -1, width)
    grad_in = final[:, :cut].reshape(rows, width) + dy.astype(f32)
    grad_qkv = tn(act1_cols, late)
    hidden_out, grad_qkv = after(gather_t((branch + out_sum).astype(bf16)), grad_qkv)
    hidden_out = hidden_out.astype(f32) + xf
    flat = final[:, cut : cut + lines].reshape(nt_, lines * width)
    gains, start = [], 0
    for size in sizes:
        gains.append(flat[:, start : start + size].reshape(-1))
        start += size
    grad_router = gains.pop(0).reshape(-1, experts)
    grad_down = tn(hid_gated, dy_all)
    grad_out_w = tn(d_branch_cols, mixed_all)
    shape = hidden_in.shape
    return (
        hidden_out.reshape(shape),
        grad_in.reshape(shape),
        gains[0],
        gains[1],
        gains[2],
        gains[3],
        grad_qkv[:, :q_cols],
        grad_qkv[:, q_cols : q_cols + hd],
        grad_qkv[:, q_cols + hd :],
        grad_out_w,
        grad_router,
        grad_gate.reshape(w_gate.shape),
        grad_up.reshape(w_up.shape),
        grad_down.reshape(w_down.shape),
    )


def solution(mesh):
    rows = P(None, B, C, None)
    ids = P(None, B, C)
    whole = P()
    matrix = P(BC, T)
    router = P(BC, None)
    expert = P(BC, T, None)
    vector = P(BC)
    in_specs = (rows, ids, rows) + (whole,) * 5 + (matrix,) * 4 + (router,) + (expert,) * 3 + (rows,)
    out_specs = (rows, rows) + (vector,) * 4 + (matrix,) * 4 + (router,) + (expert,) * 3
    return jax.shard_map(body, mesh=mesh, in_specs=in_specs, out_specs=out_specs, check_vma=False)
```

```python
import functools

import jax
import jax.numpy as jnp
from jax import lax
from jax.experimental import pallas as pl
from jax.experimental.pallas import tpu as pltpu
from jax.sharding import PartitionSpec as P

B, C, T = "batch", "ctx", "tensor"
BC = (B, C)
ALL = (B, C, T)
f32 = jnp.float32
bf16 = jnp.bfloat16
EPS = 1e-06


def dot(a, b, ca, cb):
    return lax.dot_general(a, b, (((ca,), (cb,)), ((), ())), preferred_element_type=f32)


def nn(a, b):
    return dot(a, b, 1, 0)


def nt(a, b):
    return dot(a, b, 1, 1)


def tn(a, b):
    return dot(a, b, 0, 0)


def bdot(a, b, ca, cb):
    return lax.dot_general(a, b, (((ca,), (cb,)), ((0,), (0,))), preferred_element_type=f32)


def after(*values):
    return lax.optimization_barrier(values)


def pad_cols(v, width):
    return jnp.pad(v, ((0, 0), (0, width - v.shape[1])))


def inv_rms(v):
    return lax.rsqrt(jnp.mean(v * v, axis=-1, keepdims=True) + EPS)


def turn(v):
    half = v.shape[-1] // 2
    return jnp.concatenate([-v[..., half:], v[..., :half]], axis=-1)


def angles(positions, width):
    half = width // 2
    frequency = jnp.power(1000000.0, -(2.0 * jnp.arange(half, dtype=f32)) / width)
    phases = positions.astype(f32)[:, None] * frequency[None, :]
    phases = jnp.concatenate([phases, phases], axis=-1)
    return jnp.cos(phases), jnp.sin(phases)


def norm_back(v, r, gain, grad):
    scaled = gain * grad
    grad_v = r * scaled - v * (r * r * r) * jnp.mean(v * scaled, axis=-1, keepdims=True)
    return grad_v, grad * v * r


def heads_forward(raw, gain, cosine, sine):
    v = raw * inv_rms(raw) * gain
    return (v * cosine + turn(v) * sine).astype(bf16)


def heads_back(raw, gain, cosine, sine, grad):
    grad = grad * cosine - turn(grad) * sine
    return norm_back(raw, inv_rms(raw), gain, grad)


def gather_t(v):
    count = lax.axis_size(T)
    return lax.all_to_all(jnp.concatenate([v] * count, axis=0), T, 0, 0, tiled=True)


def sum_t(v):
    count = lax.axis_size(T)
    got = lax.all_to_all(v.astype(bf16), T, 0, 0, tiled=True)
    got = got.reshape(count, v.shape[0] // count, v.shape[1])
    return jnp.sum(got.astype(f32), axis=0)


def swap(v):
    return lax.ppermute(v, B, [(0, 1), (1, 0)])


def across(v, k):
    return lax.ppermute(v, T, [(i, i ^ k) for i in range(lax.axis_size(T))])


def add_low(*parts):
    total = parts[0].astype(f32)
    for part in parts[1:]:
        total = total + part.astype(f32)
    return total.astype(bf16)


def gather_c(v):
    count = lax.axis_size(C)
    return lax.all_to_all(jnp.concatenate([v] * count, axis=0), C, 0, 0, tiled=True)


def spread_plane(own):
    half = own.shape[0] // 2
    from_x, from_y = across(own, 1), across(own, 2)
    low, high = across(from_x[:half], 2), across(from_y[half:], 1)
    return [own, from_x, from_y, jnp.concatenate([low, high], axis=0)]


def sum_plane(own, ring, corner, held=()):
    diagonal = add_low(corner[0][0], swap(corner[1])[0])
    half = diagonal.shape[0] // 2
    ring_far = swap(ring[1])
    east = add_low(ring[0][0, :half], ring_far[0, :half])
    north = add_low(ring[0][1, half:], ring_far[1, half:])
    diagonal, east, north = after(diagonal, east, north)
    from_x, from_y = across(diagonal[:half], 1), across(diagonal[half:], 2)
    east_top, north_low = across(east, 1), across(north, 2)
    own_far = swap(own[1])
    east = add_low(ring[0][0, half:], ring_far[0, half:], from_y)
    north = add_low(ring[0][1, :half], ring_far[1, :half], from_x)
    east, north, *held = after(east, north, *held)
    east_low, north_top = across(east, 1), across(north, 2)
    top = add_low(own[0][0, :half], own_far[0, :half], east_top, north_top)
    low = add_low(own[0][0, half:], own_far[0, half:], east_low, north_low)
    return jnp.concatenate([top, low], axis=0), held


def to_features(v):
    return lax.all_to_all(v, BC, 1, 0, tiled=True)


def send_c(plane):
    count = lax.axis_size(C)
    got = lax.all_to_all(plane, C, 0, 0, tiled=True)
    return got.reshape(count, plane.shape[0] // count, plane.shape[1])


SLAB = 256


def sum_c_permute(plane):
    count = lax.axis_size(C)
    cut = plane.shape[0] // count
    c = lax.axis_index(C)
    block = lambda k: lax.dynamic_slice(plane, (((c + k) % count) * cut, 0), (cut, plane.shape[1]))
    total = block(0).astype(f32)
    for k in range(1, count):
        got = lax.ppermute(block(k), C, [(i, (i + k) % count) for i in range(count)])
        total = total + got.astype(f32)
    return total


def expert_kernel(count, first, where_ref, *refs):
    acts, dys, marks = refs[:count], refs[count : count + 2], refs[count + 2 : 2 * count + 2]
    router_ref, place_ref = refs[2 * count + 2 : 2 * count + 4]
    weights_hbm = refs[2 * count + 4 : 2 * count + 7]
    act_b, dy_b, hid_b, dg_b, du_b, din_b, mark_b = refs[-13:-6]
    gate_w, up_w, down_w = refs[-6:-3]
    in_sem, w_sem, out_sem = refs[-3:]
    sizes = [min(2, count // 2)] + [1] * (count // 2 > 2)
    outs = refs[-18 - 2 * len(sizes) : -13]
    act_all, dy_all, hid_all, dg_all, du_all = outs[:5]
    given, low_p = [], 0
    for size, to in zip(sizes * 2, outs[5:]):
        given.append((low_p, size, to))
        low_p += size
    i = pl.program_id(0)
    width = act_b.shape[2]
    hidden = gate_w.shape[0]
    src = pl.ds(pl.multiple_of(i * SLAB, SLAB), SLAB)
    base = first + i * count * SLAB
    stored = ((act_b, act_all), (dy_b, dy_all), (hid_b, hid_all), (dg_b, dg_all), (du_b, du_all))
    weights = [
        pltpu.make_async_copy(v, w, w_sem.at[k])
        for k, (v, w) in enumerate(zip(weights_hbm, (gate_w, up_w, down_w)))
    ]

    piece = pl.num_programs(0) * SLAB

    def load(k, p):
        if k == 0:
            return pltpu.make_async_copy(acts[p].at[src], act_b.at[p], in_sem.at[0, p])
        rows = pl.ds(pl.multiple_of(where_ref[count + p] * piece + i * SLAB, SLAB), SLAB)
        return pltpu.make_async_copy(dys[p // (count // 2)].at[rows], dy_b.at[p], in_sem.at[1, p])

    def stores(p):
        rows = pl.ds(pl.multiple_of(base + p * SLAB, SLAB), SLAB)
        return [
            pltpu.make_async_copy(v.at[p], to.at[rows], out_sem.at[k, p])
            for k, (v, to) in enumerate(stored)
        ]

    def give(p, place, to):
        return pltpu.make_async_copy(din_b.at[p], to.at[place, src], out_sem.at[5, p])

    load(0, 0).start()

    @pl.when(i == 0)
    def _():
        weights[0].start()
        weights[1].start()

    load(1, 0).start()

    @pl.when(i == 0)
    def _():
        weights[2].start()

    for p in range(count):
        mark_b[p] = marks[p][0]

    @pl.when(i == 0)
    def _():
        weights[0].wait()
        weights[1].wait()

    def one(p, carry):
        for k, buffer in enumerate((act_b, dy_b)):
            pltpu.make_async_copy(acts[0].at[src], buffer.at[p], in_sem.at[k, p]).wait()
        for q in range(1, count):

            @pl.when(p == q - 1)
            def _(q=q):
                load(0, q).start()
                load(1, q).start()

        act = act_b[p]
        mark = mark_b[p]
        logits = nn(act, router_ref[...])
        top = jnp.max(jnp.where(mark > 0.5, logits, -1e30), axis=1, keepdims=True)
        parts = jnp.where(mark > 0.5, jnp.exp(logits - top), 0.0)
        parts = parts / jnp.sum(parts, axis=1, keepdims=True)
        gates = jnp.where(mark > 1.5, parts, 0.0)
        high = gates.astype(bf16)
        low = (gates - high.astype(f32)).astype(bf16)

        @pl.when((p == 0) & (i == 0))
        def _():
            weights[2].wait()

        place = place_ref[...]
        wide = nn(high, place) + nn(low, place)
        gate = nt(act, gate_w[...])
        up = nt(act, up_w[...])
        dyw = nt(dy_b[p], down_w[...])
        sig = 0.5 * jnp.tanh(0.5 * gate) + 0.5
        silu = gate * sig
        hid = silu * up
        hid_b[p] = (wide * hid).astype(bf16)
        share = nt((hid * dyw).astype(bf16), place)
        d_hid = wide * dyw
        dg_b[p] = (d_hid * up * (sig + silu * (1.0 - sig))).astype(bf16)
        du_b[p] = (d_hid * silu).astype(bf16)
        din_b[p, :, width:] = jnp.where(mark > 1.5, share, 0.0).astype(bf16)
        for w in range(0, width, 512):
            cols = slice(w, w + 512)
            total = nn(dg_b[p], gate_w[:, cols]) + nn(du_b[p], up_w[:, cols])
            din_b[p, :, cols] = total.astype(bf16)
        for copy in stores(p):
            copy.start()

        for low_p, size, to in given:

            @pl.when((p >= low_p) & (p < low_p + size))
            def _(low_p=low_p, to=to):
                give(p, p - low_p, to).start()

        return carry

    lax.fori_loop(0, count, one, 0)
    for p in range(count):
        for copy in stores(p):
            copy.wait()
        for low_p, size, to in given:
            if low_p <= p < low_p + size:
                give(p, p - low_p, to).wait()


def expert_pieces(first, where, acts, dys, marks, consts, held, total_rows):
    count = len(acts)
    rows, width = acts[0].shape
    hidden = consts[2].shape[0]
    routed = consts[0].shape[1]
    left = pl.BlockSpec(memory_space=pl.ANY)
    in_specs = [left] * (count + 2)
    in_specs += [
        pl.BlockSpec((1, SLAB, routed), lambda i, w, p=p: (w[p], i, 0)) for p in range(count)
    ]
    in_specs += [
        pl.BlockSpec(v.shape, lambda i, w: (0, 0), pipeline_mode=pl.Buffered(1)) for v in consts[:2]
    ]
    in_specs += [left] * 3
    out_shape = [jax.ShapeDtypeStruct((total_rows, width), bf16)] * 2
    out_shape += [jax.ShapeDtypeStruct((total_rows, hidden), bf16)] * 3
    sizes = [min(2, count // 2)] + [1] * (count // 2 > 2)
    out_shape += [jax.ShapeDtypeStruct((size, rows, width + routed), bf16) for size in sizes * 2]
    args = [where, *acts, *dys, *([marks] * count), *consts]
    aliases = {}
    if held is not None:
        for k, v in enumerate(held):
            aliases[len(args)] = k
            args.append(v)
            in_specs.append(left)
    outs = pl.pallas_call(
        functools.partial(expert_kernel, count, first),
        grid_spec=pltpu.PrefetchScalarGridSpec(
            num_scalar_prefetch=1,
            grid=(rows // SLAB,),
            in_specs=in_specs,
            out_specs=[left] * len(out_shape),
            scratch_shapes=[pltpu.VMEM((count, SLAB, width), bf16)] * 2
            + [pltpu.VMEM((count, SLAB, hidden), bf16)] * 3
            + [pltpu.VMEM((count, SLAB, width + routed), bf16)]
            + [pltpu.VMEM((count, SLAB, routed), f32)]
            + [pltpu.VMEM((hidden, width), bf16)] * 3
            + [pltpu.SemaphoreType.DMA((2, count))]
            + [pltpu.SemaphoreType.DMA((3,))]
            + [pltpu.SemaphoreType.DMA((6, count))],
        ),
        out_shape=out_shape,
        input_output_aliases=aliases,
        compiler_params=pltpu.CompilerParams(vmem_limit_bytes=56 << 20),
        cost_estimate=pl.CostEstimate(flops=1000, bytes_accessed=1000, transcendentals=0),
    )(*args)
    return outs[:5], outs[5:]


def attend_kernel(heads, scale, raw_ref, kv_ref, bias_ref, cos_ref, sin_ref, gain_ref, q_ref, mixed_ref):
    hd = gain_ref.shape[1]
    keys, values = kv_ref[0, :, :hd], kv_ref[0, :, hd:]
    bias = bias_ref[0]
    for h in range(heads):
        cols = slice(h * hd, (h + 1) * hd)
        raw = raw_ref[:, cols]
        v = raw * inv_rms(raw) * gain_ref[...]
        q = (v * cos_ref[...] + pltpu.roll(v, hd // 2, 1) * sin_ref[...]).astype(bf16)
        q_ref[:, cols] = q
        scores = nt(q, keys) * scale + bias
        weight = jnp.exp(scores - jnp.max(scores, axis=1, keepdims=True))
        probs = weight / jnp.sum(weight, axis=1, keepdims=True)
        mixed_ref[:, cols] = nn(probs.astype(bf16), values).astype(bf16)


def attend(qkv, q_cols, window, bias, cosine, sine, gain):
    micro, reach, pair = window.shape
    hd = pair // 2
    span = qkv.shape[0] // micro
    row = lambda m: (m, 0)
    flat = lambda m: (0, 0)
    deep = lambda m: (m, 0, 0)
    return pl.pallas_call(
        functools.partial(attend_kernel, q_cols // hd, hd ** (-0.5)),
        grid=(micro,),
        in_specs=[
            pl.BlockSpec((span, q_cols), row),
            pl.BlockSpec((1, reach, pair), deep),
            pl.BlockSpec((1, span, reach), deep),
            pl.BlockSpec((span, hd), flat),
            pl.BlockSpec((span, hd), flat),
            pl.BlockSpec((1, hd), flat),
        ],
        out_specs=[pl.BlockSpec((span, q_cols), row)] * 2,
        out_shape=[jax.ShapeDtypeStruct((micro * span, q_cols), bf16)] * 2,
        compiler_params=pltpu.CompilerParams(vmem_limit_bytes=32 << 20),
        cost_estimate=pl.CostEstimate(
            flops=4 * micro * span * reach * q_cols,
            bytes_accessed=8 * micro * span * q_cols,
            transcendentals=micro * span * reach * q_cols // hd,
        ),
    )(qkv, window, bias, cosine, sine, gain)


def attend_back_kernel(heads, scale, q_ref, raw_ref, kv_ref, bias_ref, dm_ref, cos_ref, sin_ref, gain_ref, dq_ref, dkv_ref, gq_ref, rows_q, rows_m, rows_p, rows_s):
    span = q_ref.shape[0]
    hd = gain_ref.shape[1]
    keys, values = kv_ref[0, :, :hd], kv_ref[0, :, hd:]
    bias = bias_ref[0]
    cosine, sine = cos_ref[...], sin_ref[...]
    gain = gain_ref[...]

    @pl.when(pl.program_id(0) == 0)
    def _():
        gq_ref[...] = jnp.zeros_like(gq_ref)

    total = jnp.zeros((1, hd), f32)
    for h in range(heads):
        cols = slice(h * hd, (h + 1) * hd)
        lines = slice(h * span, (h + 1) * span)
        q = q_ref[:, cols]
        dm = dm_ref[:, cols]
        rows_q[lines, :] = q
        rows_m[lines, :] = dm
        scores = nt(q, keys) * scale + bias
        weight = jnp.exp(scores - jnp.max(scores, axis=1, keepdims=True))
        probs = weight / jnp.sum(weight, axis=1, keepdims=True)
        d_probs = nt(dm, values)
        d_scores = probs * (d_probs - jnp.sum(probs * d_probs, axis=1, keepdims=True))
        low = d_scores.astype(bf16)
        rows_p[lines, :] = probs.astype(bf16)
        rows_s[lines, :] = low
        d_q = nn(low, keys) * scale
        grad = d_q * cosine - pltpu.roll(d_q, hd // 2, 1) * sine
        raw = raw_ref[:, cols]
        d_raw, gain_rows = norm_back(raw, inv_rms(raw), gain, grad)
        dq_ref[:, cols] = d_raw.astype(bf16)
        total = total + jnp.sum(gain_rows, axis=0, keepdims=True)
    gq_ref[...] += total
    dkv_ref[0, :, :hd] = (tn(rows_s[...], rows_q[...]) * scale).astype(bf16)
    dkv_ref[0, :, hd:] = tn(rows_p[...], rows_m[...]).astype(bf16)


def attend_back(q, qkv, window, bias, d_mixed, cosine, sine, gain):
    micro, reach, pair = window.shape
    hd = pair // 2
    span, q_cols = q.shape[0] // micro, q.shape[1]
    heads = q_cols // hd
    row = lambda m: (m, 0)
    flat = lambda m: (0, 0)
    deep = lambda m: (m, 0, 0)
    return pl.pallas_call(
        functools.partial(attend_back_kernel, heads, hd ** (-0.5)),
        grid=(micro,),
        in_specs=[
            pl.BlockSpec((span, q_cols), row),
            pl.BlockSpec((span, q_cols), row),
            pl.BlockSpec((1, reach, pair), deep),
            pl.BlockSpec((1, span, reach), deep),
            pl.BlockSpec((span, q_cols), row),
            pl.BlockSpec((span, hd), flat),
            pl.BlockSpec((span, hd), flat),
            pl.BlockSpec((1, hd), flat),
        ],
        out_specs=[
            pl.BlockSpec((span, q_cols), row),
            pl.BlockSpec((1, reach, pair), deep),
            pl.BlockSpec((1, hd), flat),
        ],
        out_shape=[
            jax.ShapeDtypeStruct(q.shape, bf16),
            jax.ShapeDtypeStruct(window.shape, bf16),
            jax.ShapeDtypeStruct((1, hd), f32),
        ],
        scratch_shapes=[pltpu.VMEM((heads * span, hd), bf16)] * 2
        + [pltpu.VMEM((heads * span, reach), bf16)] * 2,
        compiler_params=pltpu.CompilerParams(vmem_limit_bytes=32 << 20),
        cost_estimate=pl.CostEstimate(
            flops=10 * micro * heads * span * reach * hd,
            bytes_accessed=10 * micro * span * q_cols,
            transcendentals=micro * heads * span * reach,
        ),
    )(q, qkv, window, bias, d_mixed, cosine, sine, gain)


def turn_back_kernel(experts, got_ref, act_ref, mid_ref, dy_ref, chosen_ref, router_ref, gain_ref, dn_ref, low_ref, dl_ref, gain_out):
    width = mid_ref.shape[1]
    total = got_ref[0].astype(f32)
    for k in range(1, got_ref.shape[0]):
        total = total + got_ref[k].astype(f32)
    d_gates = total[:, width:]
    router = router_ref[...]
    chosen = chosen_ref[...]
    logits = nn(act_ref[...], router)
    real = lax.broadcasted_iota(jnp.int32, logits.shape, 1) < experts
    logits = jnp.where(real, logits, -1e30)
    weight = jnp.exp(logits - jnp.max(logits, axis=1, keepdims=True))
    probs = weight / jnp.sum(weight, axis=1, keepdims=True)
    picked = probs * chosen
    picked_sum = jnp.sum(picked, axis=1, keepdims=True)
    lean = jnp.sum(d_gates * picked / picked_sum, axis=1, keepdims=True)
    c_grad = chosen * (d_gates - lean) / picked_sum
    d_logits = probs * (c_grad - jnp.sum(probs * c_grad, axis=1, keepdims=True))
    d_logits = jnp.where(real, d_logits, 0.0).astype(bf16)
    dl_ref[...] = d_logits
    d_act = total[:, :width] + nt(d_logits, router)
    middle = mid_ref[...]
    d_norm, gain_rows = norm_back(middle, inv_rms(middle), gain_ref[...], d_act)
    dn_ref[...] = d_norm
    low_ref[...] = (dy_ref[...].astype(f32) + d_norm).astype(bf16)
    gain_out[...] = jnp.sum(gain_rows, axis=0, keepdims=True)


def turn_back(experts, got, act2, middle, dy_slice, chosen, router, gain):
    cut, width = middle.shape
    routed = router.shape[1]
    return pl.pallas_call(
        functools.partial(turn_back_kernel, experts),
        out_shape=[
            jax.ShapeDtypeStruct((cut, width), f32),
            jax.ShapeDtypeStruct((cut, width), bf16),
            jax.ShapeDtypeStruct((cut, routed), bf16),
            jax.ShapeDtypeStruct((1, width), f32),
        ],
        compiler_params=pltpu.CompilerParams(vmem_limit_bytes=32 << 20),
        cost_estimate=pl.CostEstimate(
            flops=4 * cut * width * routed, bytes_accessed=20 * cut * width, transcendentals=cut * routed
        ),
    )(got, act2, middle, dy_slice, chosen, router, gain)


def out_kernel(where_ref, hid_ref, down_ref, near_ref, far_ref):
    p = pl.program_id(0)
    value = nn(hid_ref[...], down_ref[...]).astype(bf16)

    @pl.when(p % 2 == 0)
    def _():
        near_ref[0] = value

    @pl.when(p % 2 == 1)
    def _():
        far_ref[0] = value


def out_pieces(hid, down, blocks, homes, piece_rows):
    hidden, width = down.shape
    count = lax.axis_size(T)
    n_slab = piece_rows // SLAB
    where = jnp.concatenate([jnp.asarray(blocks, jnp.int32), homes])
    n = len(blocks)
    home = lambda p, w: (w[n + p // 2], (p // 2) % n_slab, 0)
    return pl.pallas_call(
        out_kernel,
        grid_spec=pltpu.PrefetchScalarGridSpec(
            num_scalar_prefetch=1,
            grid=(n,),
            in_specs=[
                pl.BlockSpec((SLAB, hidden), lambda p, w: (w[p], 0)),
                pl.BlockSpec((hidden, width), lambda p, w: (0, 0), pipeline_mode=pl.Buffered(1)),
            ],
            out_specs=[pl.BlockSpec((1, SLAB, width), home)] * 2,
        ),
        out_shape=[jax.ShapeDtypeStruct((count, piece_rows, width), bf16)] * 2,
        compiler_params=pltpu.CompilerParams(vmem_limit_bytes=32 << 20),
        cost_estimate=pl.CostEstimate(flops=1000, bytes_accessed=1000, transcendentals=0),
    )(where, hid, down)


def sum_t_permute(v):
    count = lax.axis_size(T)
    cut = v.shape[0] // count
    t = lax.axis_index(T)
    low = v.astype(bf16)
    block = lambda k: lax.dynamic_slice(low, ((t ^ k) * cut, 0), (cut, v.shape[1]))
    total = block(0).astype(f32)
    for k in range(1, count):
        total = total + across(block(k), k).astype(f32)
    return total


def body(
    hidden_in,
    segment_ids,
    expert_ids,
    capacity,
    norm_attn,
    norm_ffn,
    norm_query,
    norm_key,
    w_query,
    w_key,
    w_value,
    w_out,
    w_router,
    w_gate,
    w_up,
    w_down,
    grad_out,
):
    micro, _, span, width = hidden_in.shape
    rows = micro * span
    hd = norm_query.shape[0]
    topk = expert_ids.shape[3]
    experts = w_router.shape[1]
    mine = w_gate.shape[0]
    nb, nc, nt_ = lax.axis_size(B), lax.axis_size(C), lax.axis_size(T)
    sources = nb * nc
    cut = rows // nt_
    b, c, t = lax.axis_index(B), lax.axis_index(C), lax.axis_index(T)
    place = b * nc + c
    seq = span * nc
    back = (seq // 2 - 1 + span - 1) // span
    heads = w_query.shape[1] // hd
    q_cols = heads * hd
    scale = hd ** (-0.5)
    routed = -(-experts // 128) * 128

    x = hidden_in.reshape(rows, width)
    dy = grad_out.reshape(rows, width)

    w_qkv = lax.all_gather(
        jnp.concatenate([w_query, w_key, w_value], axis=1), BC, axis=0, tiled=True
    )
    ids_own = expert_ids.reshape(rows, topk).T
    info = jnp.concatenate([ids_own, segment_ids.reshape(1, rows)], axis=0)
    info = jnp.pad(info, ((0, -(-(topk + 1) // 8) * 8 - topk - 1), (0, 0)))
    tall = info.shape[0]
    info = lax.all_to_all(jnp.concatenate([info] * sources, axis=0), BC, 0, 0, tiled=True)
    info = info.reshape(sources, tall, rows)
    ids_all = info[:, :topk]
    seg_all = info[:, topk].reshape(nb, nc, micro, span)
    local = place * mine + jnp.arange(mine)
    hot = jnp.sum((ids_all[:, :, None, :] == local[None, None, :, None]).astype(f32), axis=1)
    hot = hot.reshape(sources, mine, micro, span)
    upper = (jnp.arange(span)[:, None] < jnp.arange(span)[None, :]).astype(bf16)
    within = nn(hot.astype(bf16).reshape(-1, span), upper).reshape(hot.shape)
    totals = jnp.sum(hot, axis=-1)
    earlier = jnp.arange(sources)[:, None] < jnp.arange(sources)[None, :]
    before = jnp.sum(jnp.where(earlier[:, :, None, None], totals[:, None], 0.0), axis=0)
    rank = within + before[..., None]
    room = lax.dynamic_slice(capacity, (place * mine,), (mine,)).astype(f32)
    kept = jnp.where(rank < room[None, :, None, None], hot, 0.0)
    kept = kept.reshape(nb, nc, mine, nt_, cut).transpose(0, 3, 1, 4, 2).reshape(-1, mine)
    ids_rows = ids_all.reshape(nb, nc, topk, nt_, cut).transpose(0, 3, 1, 4, 2).reshape(-1, topk)
    names = jnp.arange(routed)
    marks = jnp.sum((ids_rows[:, :, None] == names).astype(f32), axis=1)
    for e in range(mine):
        marks = marks + jnp.where(names[None, :] == place * mine + e, kept[:, e : e + 1], 0.0)
    piece_rows = nc * cut
    marks = marks.reshape(nb * nt_, piece_rows, routed)
    total_rows = nb * nt_ * piece_rows
    ids_slice = lax.dynamic_slice(expert_ids.reshape(rows, topk), (t * cut, 0), (cut, topk))
    chosen = jnp.sum((ids_slice[:, :, None] == names).astype(f32), axis=1)

    xf = x.astype(f32)
    act1 = (xf * inv_rms(xf) * norm_attn).astype(bf16)
    positions = c * span + jnp.arange(span)
    cosine, sine = angles(positions, hd)
    cosine = jnp.concatenate([cosine] * micro, axis=0)
    sine = jnp.concatenate([sine] * micro, axis=0)
    act1_slice = lax.dynamic_slice(act1, (t * cut, 0), (cut, width))
    own_cols = width // sources

    def columns(v):
        v = gather_t(v).reshape(nt_, sources, cut, own_cols)
        return v.transpose(1, 0, 2, 3).reshape(-1, own_cols)

    act1_cols = columns(to_features(act1_slice))
    w_or = jnp.concatenate([w_out, pad_cols(w_router, routed)], axis=1)
    dy_slice = lax.dynamic_slice(dy, (t * cut, 0), (cut, width))
    w_qkv, w_or, marks, act1, act1_cols, cosine, sine, dy_tied = after(
        w_qkv, w_or, marks, act1, act1_cols, cosine, sine, dy_slice
    )
    w_or = lax.all_gather(w_or, BC, axis=0, tiled=True)
    dy_own = gather_c(dy_tied)
    n_slab = piece_rows // SLAB
    groups = ((0,), 6 * piece_rows), ((1, 2, 3), 0)
    hidden = mine * w_gate.shape[1]
    gate_w = w_gate.reshape(hidden, width)
    up_w = w_up.reshape(hidden, width)
    down_w = w_down.reshape(hidden, width)
    qkv = nn(act1, w_qkv)
    k_raw = qkv[:, q_cols : q_cols + hd]
    k = heads_forward(k_raw, norm_key, cosine, sine)
    kv = jnp.concatenate([k, qkv[:, q_cols + hd :].astype(bf16)], axis=1)
    blocks = [
        lax.ppermute(kv, C, [(i, i + s) for i in range(nc - s)]) for s in range(back, 0, -1)
    ]
    window = jnp.stack(blocks + [kv]).reshape(back + 1, micro, span, 2 * hd)
    window = window.transpose(1, 0, 2, 3).reshape(micro, (back + 1) * span, 2 * hd)
    seg_seq = lax.dynamic_index_in_dim(seg_all, b, 0, False)
    seg_seq = jnp.pad(seg_seq, ((back, 0), (0, 0), (0, 0)), constant_values=-1)
    seg_win = lax.dynamic_slice(seg_seq, (c, 0, 0), (back + 1, micro, span))
    seg_win = seg_win.transpose(1, 0, 2).reshape(micro, -1)
    seg_own = segment_ids.reshape(micro, span)
    allowed = (seg_own[:, :, None] == seg_win[:, None, :]) & (
        jnp.arange((back + 1) * span)[None, None, :] <= back * span + jnp.arange(span)[None, :, None]
    )
    bias = jnp.where(allowed, 0.0, -1e30)
    side = jnp.where(jnp.arange(hd) < hd // 2, -1.0, 1.0)
    cos_own, sin_own = cosine[:span], sine[:span] * side
    q, mixed = attend(qkv, q_cols, window, bias, cos_own, sin_own, norm_query[None])
    w_or, dy_own, mixed = after(w_or, dy_own, mixed)
    dy_plane = lax.all_gather(dy_own, T, axis=0, tiled=True)
    out_w = w_or[:, :q_cols]
    router_wide = w_or[:, q_cols:]
    branch = sum_t_permute(nt(mixed, out_w))
    x_slice = lax.dynamic_slice(x, (t * cut, 0), (cut, width)).astype(f32)
    middle = x_slice + branch
    r2 = inv_rms(middle)
    act2 = (middle * r2 * norm_ffn).astype(bf16)
    act2_own = gather_c(act2)
    mixed_later, act2_own, router_wide = after(mixed, act2_own, router_wide)
    mixed_all = lax.all_gather(mixed_later, BC, axis=0, tiled=True)

    places = (
        jnp.arange(routed)[:, None] == place * mine + jnp.arange(hidden)[None, :] // w_gate.shape[1]
    ).astype(bf16)
    consts = (router_wide, places, gate_w, up_w, down_w)

    def experts_on(group, base, near, dys, held):
        pairs = [(side, k) for side in (0, 1) for k in group]
        where = [(b ^ side) * nt_ + (t ^ k) for side, k in pairs]
        where += [(t ^ k) * (dys[0].shape[0] // (nt_ * piece_rows)) for side, k in pairs]
        acts = near + [swap(v) for v in near]
        return expert_pieces(base, jnp.stack(where), acts, dys, marks, consts, held, total_rows)

    half = piece_rows // 2
    from_x, from_y = across(act2_own, 1), across(act2_own, 2)
    held, own_sums = experts_on((0,), 6 * piece_rows, [act2_own], [dy_own, swap(dy_own)], None)
    *held, from_x, from_y, dy_plane = after(*held, from_x, from_y, dy_plane)
    low, high = across(from_x[:half], 2), across(from_y[half:], 1)
    corner = jnp.concatenate([low, high], axis=0)
    held, sums = experts_on((1, 2, 3), 0, [from_x, from_y, corner], [dy_plane, swap(dy_plane)], held)
    ring_sums, corner_sums = sums[0::2], sums[1::2]
    act_all, dy_all, hid_gated, d_gate, d_up = held
    d_in_plane, (hid_later, act2_later) = sum_plane(
        own_sums, ring_sums, corner_sums, (hid_gated, act2)
    )
    blocks, homes = [], []
    for g, start in groups:
        for n, k in enumerate(g):
            for i in range(n_slab):
                first = start // SLAB + i * 2 * len(g) + n
                blocks += [first, first + len(g)]
                homes.append(t ^ k)
    out_near, out_far = out_pieces(hid_later, down_w, blocks, jnp.stack(homes), piece_rows)
    d_in_plane, out_near, out_far, mixed_all = after(d_in_plane, out_near, out_far, mixed_all)
    d_in_got = send_c(d_in_plane)
    out_chip = add_low(out_near, swap(out_far)).reshape(-1, width)
    grad_up = tn(d_up, act_all)
    d_in_got, grad_up, out_chip = after(d_in_got, grad_up, out_chip)

    d_norm, d_branch_slice, d_logits, gain_ffn = turn_back(
        experts, d_in_got, act2_later, middle, dy_slice, chosen, router_wide, norm_ffn[None]
    )
    d_branch = gather_t(d_branch_slice)
    grad_gate = tn(d_gate, act_all)
    d_branch, grad_gate, act2_late, d_logits, out_chip, d_branch_slice = after(
        d_branch, grad_gate, act2_later, d_logits, out_chip, d_branch_slice
    )
    out_plane = lax.psum_scatter(out_chip, T, scatter_dimension=0, tiled=True)
    d_branch_part = to_features(d_branch_slice)
    devices = sources * nt_
    router_part = tn(act2_late, d_logits)[:, :experts]

    d_mixed = nn(d_branch, out_w).astype(bf16)
    d_mixed, d_branch_part = after(d_mixed, d_branch_part)
    d_branch_cols = columns(d_branch_part)
    d_q, d_window, gain_q = attend_back(
        q, qkv, window, bias, d_mixed, cos_own, sin_own, norm_query[None]
    )
    d_kv = d_window.reshape(micro, back + 1, span, 2 * hd)
    d_kv_own = d_kv[:, back].reshape(rows, 2 * hd).astype(f32)
    for s in range(1, back + 1):
        piece = d_kv[:, back - s].reshape(rows, 2 * hd)
        d_kv_own = d_kv_own + lax.ppermute(piece, C, [(i + s, i) for i in range(nc - s)]).astype(f32)
    d_k_raw, gain_k_rows = heads_back(k_raw, norm_key, cosine, sine, d_kv_own[:, :hd])
    gain_k = jnp.sum(gain_k_rows, axis=0)
    d_qkv = jnp.concatenate([d_q, d_k_raw.astype(bf16), d_kv_own[:, hd:].astype(bf16)], axis=1)
    late = lax.all_gather(d_qkv, BC, axis=0, tiled=True)
    d_act1_part = nt(d_qkv, w_qkv)
    gain_attn = jnp.sum(d_act1_part * (xf * inv_rms(xf)), axis=0)
    d_act1, d_branch_cols = after(sum_t_permute(d_act1_part), d_branch_cols)
    d_norm1, _ = norm_back(x_slice, inv_rms(x_slice), norm_attn, d_act1)

    pieces = [v.reshape(devices, -1) for v in (router_part, gain_attn, gain_ffn, gain_q, gain_k)]
    sizes = [v.shape[1] for v in pieces]
    flat = jnp.concatenate(pieces, axis=1).astype(bf16)
    flat = lax.all_to_all(pad_cols(flat, -(-flat.shape[1] // 128) * 128), ALL, 0, 0, tiled=True)
    flat = jnp.sum(flat.astype(f32), axis=0, keepdims=True)
    lines = -(-flat.shape[1] // width)
    flat = pad_cols(flat, lines * width).reshape(lines, width)
    flat = jnp.pad(flat, ((0, -lines % 16), (0, 0)))
    final = jnp.concatenate([d_norm + d_norm1, flat], axis=0).astype(bf16)
    final, out_plane, dy_all, mixed_all = after(final, out_plane, dy_all, mixed_all)
    out_sum = sum_c_permute(out_plane)
    final = gather_t(final).astype(f32).reshape(nt_, -1, width)
    grad_in = final[:, :cut].reshape(rows, width) + dy.astype(f32)
    grad_qkv = tn(act1_cols, late)
    hidden_out, grad_qkv = after(gather_t((branch + out_sum).astype(bf16)), grad_qkv)
    hidden_out = hidden_out.astype(f32) + xf
    flat = final[:, cut : cut + lines].reshape(nt_, lines * width)
    gains, start = [], 0
    for size in sizes:
        gains.append(flat[:, start : start + size].reshape(-1))
        start += size
    grad_router = gains.pop(0).reshape(-1, experts)
    grad_down = tn(hid_gated, dy_all)
    grad_out_w = tn(d_branch_cols, mixed_all)
    shape = hidden_in.shape
    return (
        hidden_out.reshape(shape),
        grad_in.reshape(shape),
        gains[0],
        gains[1],
        gains[2],
        gains[3],
        grad_qkv[:, :q_cols],
        grad_qkv[:, q_cols : q_cols + hd],
        grad_qkv[:, q_cols + hd :],
        grad_out_w,
        grad_router,
        grad_gate.reshape(w_gate.shape),
        grad_up.reshape(w_up.shape),
        grad_down.reshape(w_down.shape),
    )


def solution(mesh):
    rows = P(None, B, C, None)
    ids = P(None, B, C)
    whole = P()
    matrix = P(BC, T)
    router = P(BC, None)
    expert = P(BC, T, None)
    vector = P(BC)
    in_specs = (rows, ids, rows) + (whole,) * 5 + (matrix,) * 4 + (router,) + (expert,) * 3 + (rows,)
    out_specs = (rows, rows) + (vector,) * 4 + (matrix,) * 4 + (router,) + (expert,) * 3
    return jax.shard_map(body, mesh=mesh, in_specs=in_specs, out_specs=out_specs, check_vma=False)
```
